32 devices in a mesh: gx: 8 (over y, x, core), gy: 4 (over z).
Axes of the slice: x: 2, y: 2, z: 4, core: 2. Of those that a mesh axis runs over, the one named last changes fastest.
Arguments:
- adjoint_source: float32 [4, 64, 256, 512], P(None, 'gx', 'gy'), may hold values from -40 to 40, as said below
- conductivity: float32 [64, 256, 512], P('gx', 'gy'), may hold values from 0.1 to 10
- electrodes: int32 [4], replicated, may hold values from 0 to 16383
Outputs:
- solution_field: float32 [4, 64, 256, 512], P(None, 'gx', 'gy')
- residual: float32 [4, 64, 256, 512], P(None, 'gx', 'gy')
The draws below stay inside these ranges and needn't reach their ends.
Inputs may be any that keep to these rules, and one draw needn't show every extreme that they name: `electrodes`: each entry is a surface cell index, its first coordinate times 256 plus its second. `adjoint_source`: drawn afresh cell by cell.
All inputs are finite; a program needn't handle non-finite values.
Results may differ from the reference program's by a relative error of at most 0.0003.
Values sent between devices are 32-bit elements; how exact they have to be, the bound alone decides.
A program may use at most 128 MiB of HBM per device.

```python
import math
import jax
import jax.numpy as jnp
from jax import lax

CZ = 512
SOURCES = 4
ITERS = 2
NX = 64
NY = 256


def draw_adjoint_source(key, part):
    key_base, key_column, key_cell = jax.random.split(key, 3)
    shape = (SOURCES, NX, NY, CZ)
    column_draw = jax.random.uniform(key_column, (SOURCES,), jnp.float32, 0.0, 1.0)
    column_level = (jnp.arange(SOURCES, dtype=jnp.float32) + column_draw) / SOURCES
    column = jnp.exp(column_level * math.log(10.0)).reshape(SOURCES, 1, 1, 1)
    cell = jnp.exp(jax.random.uniform(key_cell, (1, NX, NY, CZ), jnp.float32, 0.0, math.log(10.0)))
    position = jnp.arange(NX, dtype=jnp.float32) / max(NX - 1, 1)
    base = jax.random.truncated_normal(key_base, -6.0, 6.0, shape, jnp.float32)
    rise = jnp.exp(position * math.log(3.0))
    values = 0.1 * base * column * cell * rise[None, :, None, None]
    return jnp.clip(values, -40.0, 40.0)


def with_ends(values, rng, least, largest):
    dims = values.shape
    spot = [jax.random.randint(jax.random.fold_in(rng, axis), (), 0, dims[axis]) for axis in range(len(dims))]
    values = values.at[tuple(spot)].set(least)
    longest = dims.index(max(dims))
    spot[longest] = (spot[longest] + 1) % dims[longest]
    return values.at[tuple(spot)].set(largest)


def shard_levels(stream_key, dims, shards, least, high):
    gain = 1.0
    for dim, shards_of in shards:
        steps = jax.random.uniform(jax.random.fold_in(jax.random.fold_in(stream_key, 6), dim), (shards_of,), jnp.float32, least / len(shards), high / len(shards))
        gain = gain * jnp.repeat(jnp.exp(steps), dims[dim] // shards_of).reshape((-1,) + (1,) * (len(dims) - 1 - dim))
    return gain


def setup_inputs(seed: int = 0) -> dict:
    arg_keys = jax.random.split(jax.random.key(seed), 4)
    adjoint_source = draw_adjoint_source(jax.random.fold_in(arg_keys[3], 71), 0)
    conductivity = jnp.clip(jnp.exp(math.log(10.0) - 4.6051702 * jax.random.uniform(arg_keys[1], (NX, NY, CZ), jnp.float32) ** shard_levels(arg_keys[1], (NX, NY, CZ), ((0, 8), (1, 4)), -0.2, 0.2)), 0.1, 10.0)
    electrodes = with_ends(jax.random.randint(arg_keys[2], (SOURCES,), 0, NX * NY), jax.random.fold_in(arg_keys[2], 1), 0, (NX * NY) - 1).astype(jnp.int32)
    return dict(adjoint_source=adjoint_source, conductivity=conductivity, electrodes=electrodes)


def face_coefficients(padded):
    center = padded[1:-1, 1:-1, 1:-1]

    def face(neighbour):
        return jnp.where(neighbour > 0.0, 0.5 * (center + neighbour), center)
    return (face(padded[2:, 1:-1, 1:-1]), face(padded[:-2, 1:-1, 1:-1]), face(padded[1:-1, 2:, 1:-1]), face(padded[1:-1, :-2, 1:-1]), face(padded[1:-1, 1:-1, 2:]), face(padded[1:-1, 1:-1, :-2]))

def apply_operator(padded, coeffs):
    center = padded[:, 1:-1, 1:-1, 1:-1]
    others = (padded[:, 2:, 1:-1, 1:-1], padded[:, :-2, 1:-1, 1:-1], padded[:, 1:-1, 2:, 1:-1], padded[:, 1:-1, :-2, 1:-1], padded[:, 1:-1, 1:-1, 2:], padded[:, 1:-1, 1:-1, :-2])
    total = jnp.zeros(center.shape, jnp.float32)
    for coeff, other in zip(coeffs, others):
        total = total + coeff[None] * (center - other)
    return total

def gram(left, right):
    return jnp.einsum('ixyz,jxyz->ij', left, right, precision=lax.Precision.HIGHEST)

def combine(matrix, block):
    return jnp.einsum('ij,ixyz->jxyz', matrix, block, precision=lax.Precision.HIGHEST)

def small_solve(spd, rhs):
    factor = jnp.linalg.cholesky(spd)
    return jax.scipy.linalg.cho_solve((factor, True), rhs)

def reference(adjoint_source, conductivity, electrodes):
    coeffs = face_coefficients(jnp.pad(conductivity, 1))
    current = math.sqrt(NX * NY * CZ)
    row_x = (electrodes // NY).astype(jnp.int32)
    row_y = (electrodes % NY).astype(jnp.int32)
    mark_x = (jnp.arange(NX, dtype=jnp.int32)[None, :] == row_x[:, None]).astype(jnp.float32)
    mark_y = (jnp.arange(NY, dtype=jnp.int32)[None, :] == row_y[:, None]).astype(jnp.float32)
    spike = current * (mark_x[:, :, None] * mark_y[:, None, :])
    right_side = adjoint_source.at[:, :, :, 0].add(spike)
    solution_field = jnp.zeros_like(right_side)
    residual = right_side
    direction = right_side
    norm_now = gram(residual, residual)
    for step in range(ITERS):
        padded = jnp.pad(direction, ((0, 0), (1, 1), (1, 1), (1, 1)))
        image = apply_operator(padded, coeffs)
        curvature = gram(direction, image)
        alpha = small_solve(curvature, norm_now)
        solution_field = solution_field + combine(alpha, direction)
        residual = residual - combine(alpha, image)
        if step + 1 < ITERS:
            norm_next = gram(residual, residual)
            beta = small_solve(norm_now, norm_next)
            direction = residual + combine(beta, direction)
            norm_now = norm_next
    return (solution_field, residual)
```

```python
import functools
import math

import jax
import jax.numpy as jnp
from jax import lax
from jax.experimental import pallas as pl
from jax.experimental.pallas import tpu as pltpu
from jax.sharding import PartitionSpec as P

MESH = pl.DeviceIdType.MESH
F = 4
PAIRS = [(i, j) for i in range(F) for j in range(i, F)]
NP = len(PAIRS)
TILE = 8
GRANT_A = 16 * 1024 * 1024
GRANT_B = 5 * 1024 * 1024
LANES = 128


def remote(src, dst, send, recv, axis, index):
    return pltpu.make_async_remote_copy(
        src_ref=src, dst_ref=dst, send_sem=send, recv_sem=recv,
        device_id={axis: index}, device_id_type=MESH,
    )


def operator_kernel(
    nx, ny, current, adj, sig, elec, R, Q, W, sums,
    S, wt, qx, relay_r, relay_s, relay_q, acc, part_x, part_y,
    local, xs, xr, hr, fs, ys, yr, ax_s, ax_r, ay_s, ay_r,
):
    cx, cy, cz = sig.shape
    Z = cz // LANES
    T = cy // TILE
    total_y = ny * cy
    mx, my = lax.axis_index("gx"), lax.axis_index("gy")
    barrier = pltpu.get_barrier_semaphore()
    rows = pl.ds(TILE, cy)
    inner = pl.ds(1, cx)

    loads = []
    for z in range(Z):
        at = pl.ds(z * LANES, LANES)
        loads.append(pltpu.make_async_copy(adj.at[:, :, :, at], R.at[:, inner, z, rows, :], local.at[0, z]))
        loads.append(pltpu.make_async_copy(sig.at[:, :, at], S.at[inner, z, rows, :], local.at[1, z]))
    for load in loads:
        load.start()
    for axis, me, n in (("gx", mx, nx), ("gy", my, ny)):
        for d in range(1, n):
            pl.semaphore_signal(
                barrier, inc=1, device_id={axis: lax.rem(me + d, n)}, device_id_type=MESH
            )

    has_lo, has_hi = mx > 0, mx < nx - 1
    below, above = jnp.maximum(mx - 1, 0), jnp.minimum(mx + 1, nx - 1)
    y_lo, y_hi = my > 0, my < ny - 1
    left, right = jnp.maximum(my - 1, 0), jnp.minimum(my + 1, ny - 1)

    half = Z // 2
    mid = nx // 2
    relaying = nx >= 4
    order = [z for k in range(half) for z in (k, Z - 1 - k)] + ([half] if Z % 2 else [])
    first_up = [z for z in order if z < half]
    first_dn = [z for z in order if z >= half]
    by_relay = [z for k, z in enumerate(order) if relaying and (k // 2) % 2 == 1]
    slot = {z: k for k, z in enumerate(by_relay)}
    up_cross, dn_cross = mx == mid - 1, mx == mid
    up_end, dn_end = mx == nx - 1, mx == 0

    def lanes(z):
        return pl.ds(z * LANES, LANES)

    def hop(d, k, z, axis_to):
        plane = cx - 1 if d == 0 else 0
        halo = 0 if d == 0 else cx + 1
        if k == 0:
            src, dst = adj.at[:, plane, :, lanes(z)], R.at[:, halo, z, rows, :]
        elif k == 1:
            src, dst = sig.at[plane, :, lanes(z)], S.at[halo, z, rows, :]
        else:
            src, dst = Q.at[:, plane, z, rows, :], qx.at[d, :, z]
        return remote(src, dst, xs.at[d, k, z], xr.at[d, k, z], "gx", axis_to)

    def to_relay(d, k, z):
        plane = cx - 1 if d == 0 else 0
        end = nx - 1 if d == 0 else 0
        if k == 0:
            src = adj.at[:, plane, :, lanes(z)]
        elif k == 1:
            src = sig.at[plane, :, lanes(z)]
        else:
            src = Q.at[:, plane, z, rows, :]
        dst = (relay_r, relay_s, relay_q)[k].at[slot[z]]
        return remote(src, dst, xs.at[d, k, z], hr.at[k, slot[z]], "gx", end)

    def from_relay(d, k, z):
        halo = 0 if d == 0 else cx + 1
        if k == 0:
            dst = R.at[:, halo, z, rows, :]
        elif k == 1:
            dst = S.at[halo, z, rows, :]
        else:
            dst = qx.at[d, :, z]
        src = (relay_r, relay_s, relay_q)[k].at[slot[z]]
        target = mid if d == 0 else mid - 1
        return remote(src, dst, fs.at[k, slot[z]], xr.at[d, k, z], "gx", target)

    sides = ((0, has_hi, above, up_cross, up_end), (1, has_lo, below, dn_cross, dn_end))

    def send(d, k, z):
        _, there, to, cross, _ = sides[d]
        if z in by_relay:
            @pl.when(there & jnp.logical_not(cross))
            def _():
                hop(d, k, z, to).start()

            @pl.when(cross)
            def _():
                to_relay(d, k, z).start()
        else:
            @pl.when(there)
            def _():
                hop(d, k, z, to).start()

    def forward(d, k, z):
        @pl.when(sides[d][4])
        def _():
            to_relay(d, k, z).wait_recv()
            from_relay(d, k, z).start()

    def arrive(d, k, z):
        hop(d, k, z, above if d == 0 else below).wait_recv()

    def y_hop(d, k):
        src_row, dst_row = (TILE + cy - 1, TILE - 1) if d == 0 else (TILE, TILE + cy)
        to = right if d == 0 else left
        if k == 0:
            src, dst = R.at[:, inner, :, src_row, :], R.at[:, inner, :, dst_row, :]
        elif k == 1:
            src, dst = S.at[inner, :, src_row, :], S.at[inner, :, dst_row, :]
        elif k == 2:
            span = pl.ds(1, cx - 2)
            src, dst = Q.at[:, span, :, src_row, :], Q.at[:, span, :, dst_row, :]
        else:
            x = 0 if k == 3 else cx - 1
            src, dst = Q.at[:, x, :, src_row, :], Q.at[:, x, :, dst_row, :]
        return remote(src, dst, ys.at[d, k], yr.at[d, k], "gy", to)

    def y_send(kinds):
        for d, there in ((0, y_hi), (1, y_lo)):
            @pl.when(there)
            def _():
                for k in kinds:
                    y_hop(d, k).start()

    def y_arrive(kinds):
        for d, there in ((0, y_lo), (1, y_hi)):
            @pl.when(there)
            def _():
                for k in kinds:
                    y_hop(d, k).wait_recv()

    pl.semaphore_wait(barrier, nx + ny - 2)
    for z in order:
        for k in (0, 1):
            send(0, k, z)
            send(1, k, z)

    acc[...] = jnp.zeros_like(acc)
    nothing = jnp.zeros((cy, LANES), jnp.float32)
    no_row = jnp.zeros((1, LANES), jnp.float32)
    for load in loads:
        load.wait()

    row_id = lax.broadcasted_iota(jnp.int32, (cy, LANES), 0)
    first = lax.broadcasted_iota(jnp.int32, (cy, LANES), 1) == 0

    def spike(x):
        cell = row_id + ((mx * cx + x - 1) * total_y + my * cy)
        for f in range(F):
            here = jnp.where(first & (cell == elec[f]), current, 0.0)
            R[f, x, 0, rows, :] = R[f, x, 0, rows, :] + here

    def loop(lo, hi, body):
        def one(k, c):
            body(k)
            return c
        lax.fori_loop(lo, hi, one, 0)

    loop(1, cx + 1, spike)
    y_send((0, 1))

    for there, halo, own in ((has_lo, 0, 1), (has_hi, cx + 1, cx)):
        @pl.when(jnp.logical_not(there))
        def _():
            for z in range(Z):
                S[halo, z, rows, :] = S[own, z, rows, :]
                for f in range(F):
                    R[f, halo, z, rows, :] = nothing

    for there, halo, own in ((y_lo, TILE - 1, TILE), (y_hi, TILE + cy, TILE + cy - 1)):
        @pl.when(jnp.logical_not(there))
        def _():
            def fill(x):
                for z in range(Z):
                    S[x + 1, z, pl.ds(halo, 1), :] = S[x + 1, z, pl.ds(own, 1), :]
                    for f in range(F):
                        R[f, x + 1, z, pl.ds(halo, 1), :] = no_row
                        Q[f, x, z, pl.ds(halo, 1), :] = no_row
            loop(0, cx, fill)

    lane = lax.broadcasted_iota(jnp.int32, (TILE, LANES), 1)
    lane_lo, lane_hi = lane == 0, lane == LANES - 1

    def beside(get, zs, edge):
        blocks, fwd, bwd = {}, {}, {}
        for z in zs:
            for n in (z - 1, z, z + 1):
                if 0 <= n < Z and n not in blocks:
                    blocks[n] = get(n)
        for z in zs:
            for n in (z - 1, z):
                if n in blocks and n not in fwd:
                    fwd[n] = pltpu.roll(blocks[n], 1, axis=1)
            for n in (z, z + 1):
                if n in blocks and n not in bwd:
                    bwd[n] = pltpu.roll(blocks[n], LANES - 1, axis=1)
        out = {}
        for z in zs:
            before = fwd[z - 1] if z > 0 else edge(blocks[z])
            after = bwd[z + 1] if z < Z - 1 else edge(blocks[z])
            out[z] = (
                blocks[z],
                jnp.where(lane_lo, before, fwd[z]),
                jnp.where(lane_hi, after, bwd[z]),
            )
        return out

    def add_grams(base, lefts, rights):
        zs = list(lefts[0])
        for k, (i, j) in enumerate(PAIRS):
            total = None
            for z in zs:
                prod = lefts[i][z] * rights[j][z]
                total = prod if total is None else total + prod
            acc[base + k] = acc[base + k] + total

    def first_tile(x, t, zs):
        y = pl.multiple_of(t * TILE, TILE)
        at, up, dn = pl.ds(y + TILE, TILE), pl.ds(y + TILE - 1, TILE), pl.ds(y + TILE + 1, TILE)
        out_at = pl.ds(y, TILE)
        weights = {}
        near = beside(lambda z: S[x, z, at, :], zs, lambda v: v)
        for z in zs:
            here, zm, zp = near[z]
            faces = [
                here + S[x - 1, z, at, :], here + S[x + 1, z, at, :],
                here + S[x, z, up, :], here + S[x, z, dn, :], here + zm, here + zp,
            ]
            diag = ((faces[0] + faces[1]) + (faces[2] + faces[3])) + (faces[4] + faces[5])
            weights[z] = [diag] + faces
            for k in range(7):
                wt[k, x - 1, z, out_at, :] = weights[z][k]
        rs, qs = [], []
        for f in range(F):
            near = beside(lambda z: R[f, x, z, at, :], zs, jnp.zeros_like)
            r, q = {}, {}
            for z in zs:
                mid_v, zm, zp = near[z]
                d, wxm, wxp, wym, wyp, wzm, wzp = weights[z]
                out = d * mid_v - wzm * zm - wzp * zp
                out = out - wxm * R[f, x - 1, z, at, :] - wxp * R[f, x + 1, z, at, :]
                out = out - wym * R[f, x, z, up, :] - wyp * R[f, x, z, dn, :]
                Q[f, x - 1, z, at, :] = out
                r[z], q[z] = mid_v, out
            rs.append(r)
            qs.append(q)
        add_grams(0, rs, rs)
        add_grams(NP, rs, qs)

    def second_tile(x, t, zs, low, high):
        y = pl.multiple_of(t * TILE, TILE)
        at, up, dn = pl.ds(y + TILE, TILE), pl.ds(y + TILE - 1, TILE), pl.ds(y + TILE + 1, TILE)
        out_at = pl.ds(y, TILE)
        qs, ws = [], []
        for f in range(F):
            near = beside(lambda z: Q[f, x - 1, z, at, :], zs, jnp.zeros_like)
            q, w = {}, {}
            for z in zs:
                mid_v, zm, zp = near[z]
                out = wt[0, x - 1, z, out_at, :] * mid_v
                out = out - wt[5, x - 1, z, out_at, :] * zm - wt[6, x - 1, z, out_at, :] * zp
                if low:
                    out = out - wt[1, x - 1, z, out_at, :] * Q[f, x - 2, z, at, :]
                if high:
                    out = out - wt[2, x - 1, z, out_at, :] * Q[f, x, z, at, :]
                out = out - wt[3, x - 1, z, out_at, :] * Q[f, x - 1, z, up, :]
                out = out - wt[4, x - 1, z, out_at, :] * Q[f, x - 1, z, dn, :]
                W[f, x - 1, z, out_at, :] = out
                q[z], w[z] = mid_v, out
            qs.append(q)
            ws.append(w)
        add_grams(2 * NP, qs, qs)
        add_grams(3 * NP, qs, ws)

    def face_tile(d, z, t, grams):
        x = 0 if d == 0 else cx - 1
        y = pl.multiple_of(t * TILE, TILE)
        at, out_at = pl.ds(y + TILE, TILE), pl.ds(y, TILE)
        face = wt[1 + d, x, z, out_at, :]
        vs = [face * qx[d, f, z, out_at, :] for f in range(F)]
        for f in range(F):
            W[f, x, z, out_at, :] = W[f, x, z, out_at, :] - vs[f]
        if grams:
            qs = [Q[f, x, z, at, :] for f in range(F)]
            for k, (i, j) in enumerate(PAIRS):
                acc[3 * NP + k] = acc[3 * NP + k] - (qs[i] * vs[j] + vs[i] * qs[j])

    def face(d, z, grams):
        @pl.when((has_lo, has_hi)[d])
        def _():
            arrive(d, 2, z)
            loop(0, T, lambda t: face_tile(d, z, t, grams))

    every = list(range(Z))

    def middle(planes, tile, *rest):
        lo, hi = planes
        loop(lo, hi, lambda x: loop(1, T - 1, lambda t: tile(x, t, every, *rest)))

    def rims(planes, tile, *rest):
        lo, hi = planes
        loop(lo, hi, lambda x: loop(0, 2, lambda k: tile(x, k * (T - 1), every, *rest)))

    def chunk(z):
        for d, there in ((0, has_lo), (1, has_hi)):
            @pl.when(there)
            def _():
                arrive(d, 0, z)
                arrive(d, 1, z)
        if z == 0:
            loop(0, 2, lambda k: spike(k * (cx + 1)))
        loop(0, 2, lambda k: loop(0, T, lambda t: first_tile(1 + k * (cx - 1), t, [z])))

    def forward_all(k_list, zs):
        for z in zs:
            for d in (0, 1):
                for k in k_list:
                    if z in by_relay:
                        forward(d, k, z)

    split = (cx + 2) // 2
    middle((2, split), first_tile)
    y_arrive((0, 1))
    forward_all((0, 1), by_relay[:1])
    rims((2, cx), first_tile)
    forward_all((0, 1), by_relay[1:])
    middle((split, cx), first_tile)
    y_send((2,))

    sent_up = sent_dn = 0
    ready = set()

    def send_ready(d, limit):
        plan = (first_up + first_dn) if d == 0 else (first_dn + first_up)
        done = sent[d]
        while len(done) < limit and plan[len(done)] in ready:
            send(d, 2, plan[len(done)])
            done.append(plan[len(done)])

    sent = ([], [])
    for n, z in enumerate(order):
        chunk(z)
        ready.add(z)
        send_ready(0, Z)
        send_ready(1, Z)
        if n == 0:
            middle((3, cx - 1), second_tile, True, True)
        if n == 1:
            y_arrive((2,))
            rims((3, cx - 1), second_tile, True, True)
    y_send((3, 4))

    ends = lambda k: 2 + k * (cx - 3)
    loop(0, 2, lambda k: loop(0, T, lambda t: second_tile(ends(k), t, every, True, True)))
    middle((1, 2), second_tile, False, True)
    middle((cx, cx + 1), second_tile, True, False)
    y_arrive((3, 4))
    rims((1, 2), second_tile, False, True)
    rims((cx, cx + 1), second_tile, True, False)

    early = [(0, z) for z in first_up] + [(1, z) for z in first_dn]
    late = [(0, z) for z in first_dn] + [(1, z) for z in first_up]
    rank = {z: n for n, z in enumerate(order)}
    early.sort(key=lambda p: rank[p[1]])
    late.sort(key=lambda p: rank[p[1]])
    for d, z in early:
        if z in by_relay:
            forward(d, 2, z)
    for d, z in early:
        face(d, z, True)

    def compact(parts):
        lane_sum = jnp.sum(parts, axis=1, keepdims=True)
        out = jnp.zeros((TILE, LANES), jnp.float32)
        for k in range(4 * NP // TILE):
            out = jnp.where(lane == k, lane_sum[k * TILE:(k + 1) * TILE], out)
        return out

    part_x[mx] = compact(jnp.sum(acc[...], axis=1))

    def exchange(buf, axis, me, n, sends, recvs):
        copies = [
            remote(buf.at[me], buf.at[me], sends.at[d - 1], recvs.at[d - 1], axis, lax.rem(me + d, n))
            for d in range(1, n)
        ]
        for copy in copies:
            copy.start()
        return copies

    def gather(buf, axis, me, n, sends, recvs):
        for d in range(1, n):
            src = lax.rem(me + n - d, n)
            remote(
                buf.at[me], buf.at[src], sends.at[d - 1], recvs.at[d - 1], axis, src
            ).wait_recv()
        total = buf[0]
        for k in range(1, n):
            total = total + buf[k]
        return total

    copies_x = exchange(part_x, "gx", mx, nx, ax_s, ax_r)
    for d, z in late:
        if z in by_relay:
            forward(d, 2, z)
    cut = len(late) // 2
    for d, z in late[:cut]:
        face(d, z, False)
    part_y[my] = gather(part_x, "gx", mx, nx, ax_s, ax_r)
    copies_y = exchange(part_y, "gy", my, ny, ay_s, ay_r)
    for d, z in late[cut:]:
        face(d, z, False)
    sums[...] = gather(part_y, "gy", my, ny, ay_s, ay_r)

    for copy in copies_x + copies_y:
        copy.wait_send()
    for d in (0, 1):
        @pl.when(sides[d][1])
        def _():
            for z in order:
                for k in range(3):
                    hop(d, k, z, sides[d][2]).wait_send()

        @pl.when(sides[d][4])
        def _():
            for z in by_relay:
                for k in range(3):
                    from_relay(d, k, z).wait_send()
    for d, there in ((0, y_hi), (1, y_lo)):
        @pl.when(there)
        def _():
            for k in range(5):
                y_hop(d, k).wait_send()


def mat(a, b):
    return [
        [sum(a[i][k] * b[k][j] for k in range(1, F)) + a[i][0] * b[0][j] for j in range(F)]
        for i in range(F)
    ]


def add(a, b):
    return [[a[i][j] + b[i][j] for j in range(F)] for i in range(F)]


def sub(a, b):
    return [[a[i][j] - b[i][j] for j in range(F)] for i in range(F)]


def turn(a):
    return [[a[j][i] for j in range(F)] for i in range(F)]


def spd_solve(a, b):
    low = [[None] * F for _ in range(F)]
    inv = [None] * F
    rest = [list(row) for row in a]
    for k in range(F):
        inv[k] = 1.0 / rest[k][k]
        for i in range(k + 1, F):
            low[i][k] = rest[i][k] * inv[k]
        for i in range(k + 1, F):
            for j in range(k + 1, i + 1):
                rest[i][j] = rest[i][j] - low[i][k] * rest[j][k]
    out = [list(row) for row in b]
    for i in range(F):
        for k in range(i):
            out[i] = [u - low[i][k] * v for u, v in zip(out[i], out[k])]
    out = [[u * inv[i] for u in out[i]] for i in range(F)]
    for i in reversed(range(F)):
        for k in range(i + 1, F):
            out[i] = [u - low[k][i] * v for u, v in zip(out[i], out[k])]
    return out


def finish_kernel(sums, r_ref, q_ref, w_ref, x_ref, e_ref, coef):
    @pl.when(pl.program_id(0) == 0)
    def _():
        lane = lax.broadcasted_iota(jnp.int32, (TILE, LANES), 1)
        rows = []
        for k in range(4 * NP // TILE):
            column = jnp.sum(jnp.where(lane == k, sums[...], 0.0), axis=1, keepdims=True)
            wide = jnp.broadcast_to(column, (TILE, LANES))
            rows.extend(wide[s:s + 1] for s in range(TILE))
        grams = []
        for g in range(4):
            m = [[None] * F for _ in range(F)]
            for k, (i, j) in enumerate(PAIRS):
                m[i][j] = m[j][i] = rows[g * NP + k]
            grams.append(m)
        s0, s1, s2, s3 = grams
        a0 = spd_solve(s1, s0)
        s1a, s2a = mat(s1, a0), mat(s2, a0)
        a0t = turn(a0)
        rr = add(sub(sub(s0, s1a), turn(s1a)), mat(a0t, s2a))
        cross = add(sub(sub(s1, s2a), turn(s2a)), mat(a0t, mat(s3, a0)))
        beta = spd_solve(s0, rr)
        curve = sub(cross, mat(turn(beta), mat(s1, beta)))
        a1 = spd_solve(curve, rr)
        m1 = add(add(a0, a1), mat(beta, a1))
        m2 = mat(a0, a1)
        for i in range(F):
            for j in range(F):
                coef[pl.ds(i * F + j, 1), :] = m1[i][j]
                coef[pl.ds(F * F + i * F + j, 1), :] = m2[i][j]

    x = pl.program_id(0)
    cy = w_ref.shape[3]
    Z = w_ref.shape[2]
    c1 = [[jnp.broadcast_to(coef[pl.ds(i * F + j, 1), :], (TILE, LANES)) for j in range(F)] for i in range(F)]
    c2 = [[jnp.broadcast_to(coef[pl.ds(F * F + i * F + j, 1), :], (TILE, LANES)) for j in range(F)] for i in range(F)]

    def tile(t, c):
        y = pl.ds(pl.multiple_of(t * TILE, TILE), TILE)
        wide_y = pl.ds(pl.multiple_of(t * TILE + TILE, TILE), TILE)
        for z in range(Z):
            at = pl.ds(z * LANES, LANES)
            rs = [r_ref[f, x + 1, z, wide_y, :] for f in range(F)]
            qs = [q_ref[f, x, z, wide_y, :] for f in range(F)]
            ws = [w_ref[f, x, z, y, :] for f in range(F)]
            for j in range(F):
                field = rs[0] * c1[0][j] - qs[0] * c2[0][j]
                left = rs[j] - qs[0] * c1[0][j] + ws[0] * c2[0][j]
                for i in range(1, F):
                    field = field + rs[i] * c1[i][j] - qs[i] * c2[i][j]
                    left = left - qs[i] * c1[i][j] + ws[i] * c2[i][j]
                x_ref[j, 0, y, at] = field + field
                e_ref[j, 0, y, at] = left
        return c

    lax.fori_loop(0, cy // TILE, tile, 0)


def shards(nx, ny, adj, sig, elec):
    cx, cy, cz = sig.shape
    Z = cz // LANES
    current = math.sqrt(nx * cx * ny * cy * cz)
    block = jax.ShapeDtypeStruct(adj.shape, jnp.float32)
    hbm = pl.BlockSpec(memory_space=pltpu.HBM)
    vmem = pl.BlockSpec(memory_space=pltpu.VMEM)
    tall = cy + 2 * TILE
    f32 = lambda *dims: pltpu.VMEM(dims, jnp.float32)
    shape = lambda *dims: jax.ShapeDtypeStruct(dims, jnp.float32)
    dma = pltpu.SemaphoreType.DMA
    adj = pltpu.with_memory_space_constraint(adj, pltpu.HBM)
    sig = pltpu.with_memory_space_constraint(sig, pltpu.HBM)
    slots = max(Z // 2, 1)
    r, q, w, sums = pl.pallas_call(
        functools.partial(operator_kernel, nx, ny, current),
        out_shape=(
            shape(F, cx + 2, Z, tall, LANES), shape(F, cx, Z, tall, LANES), shape(F, cx, Z, cy, LANES),
            shape(TILE, LANES),
        ),
        in_specs=[hbm, hbm, pl.BlockSpec(memory_space=pltpu.SMEM)],
        out_specs=(vmem, vmem, vmem, vmem),
        scratch_shapes=[
            f32(cx + 2, Z, tall, LANES),
            f32(7, cx, Z, cy, LANES),
            f32(2, F, Z, cy, LANES),
            f32(slots, F, cy, LANES),
            f32(slots, cy, LANES),
            f32(slots, F, cy, LANES),
            f32(4 * NP, TILE, LANES),
            f32(nx, TILE, LANES),
            f32(ny, TILE, LANES),
            dma((2, Z)), dma((2, 3, Z)), dma((2, 3, Z)), dma((3, slots)), dma((3, slots)),
            dma((2, 5)), dma((2, 5)),
            dma((max(nx - 1, 1),)), dma((max(nx - 1, 1),)),
            dma((max(ny - 1, 1),)), dma((max(ny - 1, 1),)),
        ],
        compiler_params=pltpu.CompilerParams(collective_id=0, has_side_effects=True, vmem_limit_bytes=GRANT_A),
    )(adj, sig, elec)
    slab = pl.BlockSpec((F, 1, cy, cz), lambda x: (0, x, 0, 0))
    return pl.pallas_call(
        finish_kernel,
        grid=(cx,),
        out_shape=(block, block),
        in_specs=[vmem, vmem, vmem, vmem],
        out_specs=(slab, slab),
        scratch_shapes=[pltpu.VMEM((2 * F * F, LANES), jnp.float32)],
        compiler_params=pltpu.CompilerParams(vmem_limit_bytes=GRANT_B),
    )(sums, r, q, w)


def solution(mesh):
    placed = (P(None, "gx", "gy", None), P("gx", "gy", None), P())
    return jax.shard_map(
        functools.partial(shards, mesh.shape["gx"], mesh.shape["gy"]),
        mesh=mesh,
        in_specs=placed,
        out_specs=(P(None, "gx", "gy", None), P(None, "gx", "gy", None)),
        check_vma=False,
    )
```

```python
import functools
import math

import jax
import jax.numpy as jnp
from jax import lax
from jax.experimental import pallas as pl
from jax.experimental.pallas import tpu as pltpu
from jax.sharding import PartitionSpec as P

MESH = pl.DeviceIdType.MESH
F = 4
PAIRS = [(i, j) for i in range(F) for j in range(i, F)]
NP = len(PAIRS)
TILE = 8
GRANT_A = 16 * 1024 * 1024
GRANT_B = 12 * 1024 * 1024
LANES = 128


def remote(src, dst, send, recv, axis, index):
    return pltpu.make_async_remote_copy(
        src_ref=src, dst_ref=dst, send_sem=send, recv_sem=recv,
        device_id={axis: index}, device_id_type=MESH,
    )


def operator_kernel(
    nx, ny, current, adj, sig, elec_ref, R, Q, W, sums,
    elec, S, wt, qx, relay_r, relay_q, acc, part_x, part_y,
    local, xs, xr, hr, fs, ys, yr, ax_s, ax_r, ay_s, ay_r,
):
    cx, cy, cz = sig.shape
    Z = cz // LANES
    T = cy // TILE
    total_y = ny * cy
    mx, my = lax.axis_index("gx"), lax.axis_index("gy")
    barrier = pltpu.get_barrier_semaphore()
    rows = pl.ds(TILE, cy)
    inner = pl.ds(1, cx)

    for axis, me, n in (("gx", mx, nx), ("gy", my, ny)):
        for d in range(1, n):
            pl.semaphore_signal(
                barrier, inc=1, device_id={axis: lax.rem(me + d, n)}, device_id_type=MESH
            )

    loads = [pltpu.make_async_copy(elec_ref, elec, local.at[2])]
    for z in range(Z):
        at = pl.ds(z * LANES, LANES)
        loads.append(pltpu.make_async_copy(adj.at[:, :, :, at], R.at[:, inner, z, rows, :], local.at[0]))
        loads.append(pltpu.make_async_copy(sig.at[:, :, at], S.at[inner, z, rows, :], local.at[1]))
    for load in loads:
        load.start()

    has_lo, has_hi = mx > 0, mx < nx - 1
    below, above = jnp.maximum(mx - 1, 0), jnp.minimum(mx + 1, nx - 1)
    y_lo, y_hi = my > 0, my < ny - 1
    left, right = jnp.maximum(my - 1, 0), jnp.minimum(my + 1, ny - 1)

    def take(ref, sem):
        pltpu.make_async_copy(ref, ref, sem).wait()

    half = Z // 2
    mid = nx // 2
    relaying = nx >= 4
    order = [z for k in range(half) for z in (k, Z - 1 - k)] + ([half] if Z % 2 else [])
    first_up = [z for k, z in enumerate(order) if k % 4 in (0, 3)]
    first_dn = [z for z in order if z not in first_up]
    relay_0 = order[Z - half:] if relaying else []
    relay_1 = order[:half] if relaying else []
    up_cross, dn_cross = mx == mid - 1, mx == mid
    up_end, dn_end = mx == nx - 1, mx == 0

    def lanes(z):
        return pl.ds(z * LANES, LANES)

    def hop(d, k, z, axis_to):
        plane = cx - 1 if d == 0 else 0
        halo = 0 if d == 0 else cx + 1
        if k == 0:
            pairs = [
                (adj.at[:, plane, :, lanes(z)], R.at[:, halo, z, rows, :]),
                (sig.at[plane, :, lanes(z)], S.at[halo, z, rows, :]),
            ]
        else:
            pairs = [(Q.at[:, plane, z, rows, :], qx.at[d, :, z])]
        return [remote(src, dst, xs.at[d], xr.at[d, k, z], "gx", axis_to) for src, dst in pairs]

    def to_relay(d, k, z):
        plane = cx - 1 if d == 0 else 0
        end = nx - 1 if d == 0 else 0
        if k == 0:
            at = relay_0.index(z)
            pairs = [
                (adj.at[:, plane, :, lanes(z)], relay_r.at[at, pl.ds(0, F)]),
                (sig.at[plane, :, lanes(z)], relay_r.at[at, F]),
            ]
        else:
            at = relay_1.index(z)
            pairs = [(Q.at[:, plane, z, rows, :], relay_q.at[at])]
        return [remote(src, dst, xs.at[d], hr.at[k, at], "gx", end) for src, dst in pairs]

    def from_relay(d, k, z):
        halo = 0 if d == 0 else cx + 1
        target = mid if d == 0 else mid - 1
        if k == 0:
            at = relay_0.index(z)
            pairs = [
                (relay_r.at[at, pl.ds(0, F)], R.at[:, halo, z, rows, :]),
                (relay_r.at[at, F], S.at[halo, z, rows, :]),
            ]
        else:
            pairs = [(relay_q.at[relay_1.index(z)], qx.at[d, :, z])]
        return [remote(src, dst, fs.at[0], xr.at[d, k, z], "gx", target) for src, dst in pairs]

    sides = ((0, has_hi, above, up_cross, up_end), (1, has_lo, below, dn_cross, dn_end))

    def start(copies):
        for copy in copies:
            copy.start()

    def send_relayed(d, k, z):
        if z in (relay_0, relay_1)[k]:
            @pl.when(sides[d][3])
            def _():
                start(to_relay(d, k, z))

    def send_direct(d, k, z):
        _, there, to, cross, _ = sides[d]
        if z in (relay_0, relay_1)[k]:
            there = there & jnp.logical_not(cross)

        @pl.when(there)
        def _():
            start(hop(d, k, z, to))

    def forward(d, k, z):
        if z in (relay_0, relay_1)[k]:
            @pl.when(sides[d][4])
            def _():
                at = (relay_0, relay_1)[k].index(z)
                take((relay_r, relay_q)[k].at[at], hr.at[k, at])
                start(from_relay(d, k, z))

    def arrive(d, k, z):
        take((relay_r, relay_q)[k].at[0], xr.at[d, k, z])

    def y_hop(d, k):
        src_row, dst_row = (TILE + cy - 1, TILE - 1) if d == 0 else (TILE, TILE + cy)
        to = right if d == 0 else left
        if k == 0:
            src, dst = R.at[:, inner, :, src_row, :], R.at[:, inner, :, dst_row, :]
        elif k == 1:
            src, dst = S.at[inner, :, src_row, :], S.at[inner, :, dst_row, :]
        elif k == 2:
            span = pl.ds(1, cx - 2)
            src, dst = Q.at[:, span, :, src_row, :], Q.at[:, span, :, dst_row, :]
        else:
            x = 0 if k == 3 else cx - 1
            src, dst = Q.at[:, x, :, src_row, :], Q.at[:, x, :, dst_row, :]
        return remote(src, dst, ys.at[d], yr.at[d, k], "gy", to)

    def y_send(kinds):
        for d, there in ((0, y_hi), (1, y_lo)):
            @pl.when(there)
            def _():
                for k in kinds:
                    y_hop(d, k).start()

    def y_arrive(kinds):
        for d, there in ((0, y_lo), (1, y_hi)):
            @pl.when(there)
            def _():
                for k in kinds:
                    y_hop(d, k).wait_recv()

    pl.semaphore_wait(barrier, nx + ny - 2)
    for z in order:
        for d in (0, 1):
            send_relayed(d, 0, z)
    for z in order:
        for d in (0, 1):
            send_direct(d, 0, z)

    acc[...] = jnp.zeros_like(acc)
    nothing = jnp.zeros((cy, LANES), jnp.float32)
    no_row = jnp.zeros((1, LANES), jnp.float32)
    take(W, local.at[0])
    take(wt.at[0], local.at[1])
    loads[0].wait()

    row_id = lax.broadcasted_iota(jnp.int32, (cy, LANES), 0)
    first = lax.broadcasted_iota(jnp.int32, (cy, LANES), 1) == 0

    def spike(x):
        cell = row_id + ((mx * cx + x - 1) * total_y + my * cy)
        for f in range(F):
            here = jnp.where(first & (cell == elec[f]), current, 0.0)
            R[f, x, 0, rows, :] = R[f, x, 0, rows, :] + here

    def loop(lo, hi, body):
        def one(k, c):
            body(k)
            return c
        lax.fori_loop(lo, hi, one, 0)

    loop(1, cx + 1, spike)
    y_send((0, 1))

    for there, halo, own in ((has_lo, 0, 1), (has_hi, cx + 1, cx)):
        @pl.when(jnp.logical_not(there))
        def _():
            for z in range(Z):
                S[halo, z, rows, :] = S[own, z, rows, :]
                for f in range(F):
                    R[f, halo, z, rows, :] = nothing

    for there, halo, own in ((y_lo, TILE - 1, TILE), (y_hi, TILE + cy, TILE + cy - 1)):
        @pl.when(jnp.logical_not(there))
        def _():
            def fill(x):
                for z in range(Z):
                    S[x + 1, z, pl.ds(halo, 1), :] = S[x + 1, z, pl.ds(own, 1), :]
                    for f in range(F):
                        R[f, x + 1, z, pl.ds(halo, 1), :] = no_row
                        Q[f, x, z, pl.ds(halo, 1), :] = no_row
            loop(0, cx, fill)

    lane = lax.broadcasted_iota(jnp.int32, (TILE, LANES), 1)
    lane_lo, lane_hi = lane == 0, lane == LANES - 1

    def beside(get, zs, edge):
        blocks, fwd, bwd = {}, {}, {}
        for z in zs:
            for n in (z - 1, z, z + 1):
                if 0 <= n < Z and n not in blocks:
                    blocks[n] = get(n)
        for z in zs:
            for n in (z - 1, z):
                if n in blocks and n not in fwd:
                    fwd[n] = pltpu.roll(blocks[n], 1, axis=1)
            for n in (z, z + 1):
                if n in blocks and n not in bwd:
                    bwd[n] = pltpu.roll(blocks[n], LANES - 1, axis=1)
        out = {}
        for z in zs:
            before = fwd[z - 1] if z > 0 else edge(blocks[z])
            after = bwd[z + 1] if z < Z - 1 else edge(blocks[z])
            out[z] = (
                blocks[z],
                jnp.where(lane_lo, before, fwd[z]),
                jnp.where(lane_hi, after, bwd[z]),
            )
        return out

    def add_grams(base, lefts, rights):
        zs = list(lefts[0])
        for k, (i, j) in enumerate(PAIRS):
            total = None
            for z in zs:
                prod = lefts[i][z] * rights[j][z]
                total = prod if total is None else total + prod
            acc[base + k] = acc[base + k] + total

    def first_tile(x, t, zs):
        y = t * TILE
        at, up, dn = pl.ds(y + TILE, TILE), pl.ds(y + TILE - 1, TILE), pl.ds(y + TILE + 1, TILE)
        out_at = pl.ds(y, TILE)
        weights = {}
        near = beside(lambda z: S[x, z, at, :], zs, lambda v: v)
        for z in zs:
            here, zm, zp = near[z]
            faces = [
                here + S[x - 1, z, at, :], here + S[x + 1, z, at, :],
                here + S[x, z, up, :], here + S[x, z, dn, :], here + zm, here + zp,
            ]
            diag = ((faces[0] + faces[1]) + (faces[2] + faces[3])) + (faces[4] + faces[5])
            weights[z] = [diag] + faces
            for k in range(7):
                wt[k, x - 1, z, out_at, :] = weights[z][k]
        rs, qs = [], []
        for f in range(F):
            near = beside(lambda z: R[f, x, z, at, :], zs, jnp.zeros_like)
            r, q = {}, {}
            for z in zs:
                mid_v, zm, zp = near[z]
                d, wxm, wxp, wym, wyp, wzm, wzp = weights[z]
                out = d * mid_v - wzm * zm - wzp * zp
                out = out - wxm * R[f, x - 1, z, at, :] - wxp * R[f, x + 1, z, at, :]
                out = out - wym * R[f, x, z, up, :] - wyp * R[f, x, z, dn, :]
                Q[f, x - 1, z, at, :] = out
                r[z], q[z] = mid_v, out
            rs.append(r)
            qs.append(q)
        add_grams(0, rs, rs)
        add_grams(NP, rs, qs)

    def second_tile(x, t, zs, low, high):
        y = t * TILE
        at, up, dn = pl.ds(y + TILE, TILE), pl.ds(y + TILE - 1, TILE), pl.ds(y + TILE + 1, TILE)
        out_at = pl.ds(y, TILE)
        qs, ws = [], []
        for f in range(F):
            near = beside(lambda z: Q[f, x - 1, z, at, :], zs, jnp.zeros_like)
            q, w = {}, {}
            for z in zs:
                mid_v, zm, zp = near[z]
                out = wt[0, x - 1, z, out_at, :] * mid_v
                out = out - wt[5, x - 1, z, out_at, :] * zm - wt[6, x - 1, z, out_at, :] * zp
                if low:
                    out = out - wt[1, x - 1, z, out_at, :] * Q[f, x - 2, z, at, :]
                if high:
                    out = out - wt[2, x - 1, z, out_at, :] * Q[f, x, z, at, :]
                out = out - wt[3, x - 1, z, out_at, :] * Q[f, x - 1, z, up, :]
                out = out - wt[4, x - 1, z, out_at, :] * Q[f, x - 1, z, dn, :]
                W[f, x - 1, z, out_at, :] = out
                q[z], w[z] = mid_v, out
            qs.append(q)
            ws.append(w)
        add_grams(2 * NP, qs, qs)
        add_grams(3 * NP, qs, ws)

    def face_tile(d, z, t, grams):
        x = 0 if d == 0 else cx - 1
        y = pl.multiple_of(t * TILE, TILE)
        at, out_at = pl.ds(y + TILE, TILE), pl.ds(y, TILE)
        face = wt[1 + d, x, z, out_at, :]
        vs = [face * qx[d, f, z, out_at, :] for f in range(F)]
        for f in range(F):
            W[f, x, z, out_at, :] = W[f, x, z, out_at, :] - vs[f]
        if grams:
            qs = [Q[f, x, z, at, :] for f in range(F)]
            for k, (i, j) in enumerate(PAIRS):
                acc[3 * NP + k] = acc[3 * NP + k] - (qs[i] * vs[j] + vs[i] * qs[j])

    def face(d, z, grams):
        @pl.when((has_lo, has_hi)[d])
        def _():
            arrive(d, 1, z)
            loop(0, T, lambda t: face_tile(d, z, t, grams))

    every = list(range(Z))

    def middle(planes, tile, *rest):
        lo, hi = planes
        def plane(x):
            for t in range(1, T - 1):
                tile(x, t, every, *rest)
        loop(lo, hi, plane)

    def rims(planes, tile, *rest):
        lo, hi = planes
        def plane(x):
            for t in (0, T - 1):
                tile(x, t, every, *rest)
        loop(lo, hi, plane)

    def chunk(z):
        for d, there in ((0, has_lo), (1, has_hi)):
            @pl.when(there)
            def _():
                arrive(d, 0, z)
        if z == 0:
            loop(0, 2, lambda k: spike(k * (cx + 1)))
        def plane(k):
            for t in range(T):
                first_tile(1 + k * (cx - 1), t, [z])
        loop(0, 2, plane)

    def forward_all(k, zs, ds=(0, 1)):
        for z in zs:
            for d in ds:
                forward(d, k, z)

    def send_image(d, z):
        send_relayed(d, 1, z)
        send_direct(d, 1, z)

    firsts = (first_up, first_dn)
    late = [(d, z) for z in order for d in (0, 1) if z not in firsts[d]]
    early = [(d, z) for z in order for d in (0, 1) if z in firsts[d]]
    split = (cx + 2) // 2
    middle((2, split), first_tile)
    middle((split, cx), first_tile)
    y_arrive((0, 1))
    forward_all(0, relay_0[:1])
    rims((2, cx), first_tile)
    y_send((2,))
    forward_all(0, relay_0[1:])
    middle((3, cx - 1), second_tile, True, True)
    for n, z in enumerate(order):
        if n == 2:
            y_arrive((2,))
            rims((3, cx - 1), second_tile, True, True)
        if n == Z - 1:
            for d in (0, 1):
                forward_all(1, [c for c in relay_1[:1] if c in firsts[d]], (d,))
        chunk(z)
        for d in (0, 1):
            if z in firsts[d]:
                send_image(d, z)
        if n == half - 1:
            for d, c in late[:half]:
                send_image(d, c)
    y_send((3, 4))
    for d in (0, 1):
        forward_all(1, [c for c in relay_1[1:] if c in firsts[d]], (d,))

    def beside_ends(k):
        for t in range(T):
            second_tile(2 + k * (cx - 3), t, every, True, True)
    loop(0, 2, beside_ends)
    middle((1, 2), second_tile, False, True)
    middle((cx, cx + 1), second_tile, True, False)
    y_arrive((3, 4))
    rims((1, 2), second_tile, False, True)
    rims((cx, cx + 1), second_tile, True, False)
    for d, z in early:
        face(d, z, True)
    for d, z in late[:half]:
        forward(d, 1, z)

    def compact(parts):
        lane_sum = jnp.sum(parts, axis=1, keepdims=True)
        out = jnp.zeros((TILE, LANES), jnp.float32)
        for k in range(4 * NP // TILE):
            out = jnp.where(lane == k, lane_sum[k * TILE:(k + 1) * TILE], out)
        return out

    part_x[mx] = compact(jnp.sum(acc[...], axis=1))

    def exchange(buf, axis, me, n, sends, recvs):
        for d in range(1, n):
            remote(buf.at[me], buf.at[me], sends.at[0], recvs.at[0], axis, lax.rem(me + d, n)).start()

    def gather(buf, n, recvs):
        if n > 1:
            take(buf.at[pl.ds(0, n - 1)], recvs.at[0])
        total = buf[0]
        for k in range(1, n):
            total = total + buf[k]
        return total

    exchange(part_x, "gx", mx, nx, ax_s, ax_r)
    for d, z in late[half:]:
        send_image(d, z)
    part_y[my] = gather(part_x, nx, ax_r)
    exchange(part_y, "gy", my, ny, ay_s, ay_r)
    for d, z in late[half:]:
        forward(d, 1, z)
    for d, z in late:
        face(d, z, False)
    sums[...] = gather(part_y, ny, ay_r)

    if nx > 1:
        take(part_x.at[pl.ds(0, nx - 1)], ax_s.at[0])
    if ny > 1:
        take(part_y.at[pl.ds(0, ny - 1)], ay_s.at[0])
    three = pl.ds(0, 3)
    for d in (0, 1):
        @pl.when(sides[d][1])
        def _():
            take(wt.at[three, three], xs.at[d])

        @pl.when((y_hi, y_lo)[d])
        def _():
            take(wt.at[0, :, :, pl.ds(0, 2 * F + 1), :], ys.at[d])

    if relaying:
        @pl.when(up_end | dn_end)
        def _():
            take(wt.at[three, three, pl.ds(0, half)], fs.at[0])


def mat(a, b):
    return [
        [sum(a[i][k] * b[k][j] for k in range(1, F)) + a[i][0] * b[0][j] for j in range(F)]
        for i in range(F)
    ]


def add(a, b):
    return [[a[i][j] + b[i][j] for j in range(F)] for i in range(F)]


def sub(a, b):
    return [[a[i][j] - b[i][j] for j in range(F)] for i in range(F)]


def turn(a):
    return [[a[j][i] for j in range(F)] for i in range(F)]


def spd_solve(a, b):
    low = [[None] * F for _ in range(F)]
    inv = [None] * F
    rest = [list(row) for row in a]
    for k in range(F):
        inv[k] = 1.0 / rest[k][k]
        for i in range(k + 1, F):
            low[i][k] = rest[i][k] * inv[k]
        for i in range(k + 1, F):
            for j in range(k + 1, i + 1):
                rest[i][j] = rest[i][j] - low[i][k] * rest[j][k]
    out = [list(row) for row in b]
    for i in range(F):
        for k in range(i):
            out[i] = [u - low[i][k] * v for u, v in zip(out[i], out[k])]
    out = [[u * inv[i] for u in out[i]] for i in range(F)]
    for i in reversed(range(F)):
        for k in range(i + 1, F):
            out[i] = [u - low[k][i] * v for u, v in zip(out[i], out[k])]
    return out


def finish_kernel(sums, r_ref, q_ref, w_ref, x_out, e_out, x_ref, e_ref, coef, sems):
    def prepare():
        lane = lax.broadcasted_iota(jnp.int32, (TILE, LANES), 1)
        rows = []
        for k in range(4 * NP // TILE):
            column = jnp.sum(jnp.where(lane == k, sums[...], 0.0), axis=1, keepdims=True)
            wide = jnp.broadcast_to(column, (TILE, LANES))
            rows.extend(wide[s:s + 1] for s in range(TILE))
        grams = []
        for g in range(4):
            m = [[None] * F for _ in range(F)]
            for k, (i, j) in enumerate(PAIRS):
                m[i][j] = m[j][i] = rows[g * NP + k]
            grams.append(m)
        s0, s1, s2, s3 = grams
        a0 = spd_solve(s1, s0)
        s1a, s2a = mat(s1, a0), mat(s2, a0)
        a0t = turn(a0)
        rr = add(sub(sub(s0, s1a), turn(s1a)), mat(a0t, s2a))
        cross = add(sub(sub(s1, s2a), turn(s2a)), mat(a0t, mat(s3, a0)))
        beta = spd_solve(s0, rr)
        curve = sub(cross, mat(turn(beta), mat(s1, beta)))
        a1 = spd_solve(curve, rr)
        m1 = add(add(a0, a1), mat(beta, a1))
        m2 = mat(a0, a1)
        zero = jnp.zeros_like(m1[0][0])
        one = zero + 1.0
        weights = []
        for j in range(F):
            weights.append([m1[i][j] + m1[i][j] for i in range(F)] + [-(m2[i][j] + m2[i][j]) for i in range(F)] + [zero] * F)
        for j in range(F):
            unit = [one if i == j else zero for i in range(F)]
            weights.append(unit + [-m1[i][j] for i in range(F)] + [m2[i][j] for i in range(F)])
        depth = 3 * F * TILE
        row_s = lax.broadcasted_iota(jnp.int32, (TILE, LANES), 0)
        blocks = [[None] * 2 for _ in weights]
        for h in range(2):
            column = lane + h * LANES
            column = jnp.where(column >= depth, column - depth, column)
            at = [column == k * TILE + row_s for k in range(3 * F)]
            for j, row in enumerate(weights):
                block = jnp.zeros((TILE, LANES), jnp.float32)
                for k in range(3 * F):
                    if row[k] is not zero:
                        block = jnp.where(at[k], jnp.broadcast_to(row[k], block.shape), block)
                blocks[j][h] = block
        full = jnp.concatenate([jnp.concatenate(pair, axis=1) for pair in blocks], axis=0)[:, :2 * depth]
        high = full.astype(jnp.bfloat16)
        low = (full - high.astype(jnp.float32)).astype(jnp.bfloat16)
        coef[...] = jnp.concatenate([high, low], axis=0)

    prepare()
    cx, Z, cy = w_ref.shape[1:4]
    wide = 2 if Z % 2 == 0 else 1

    def tile(x, t):
        y, wide_y = pl.ds(t * TILE, TILE), pl.ds(t * TILE + TILE, TILE)
        for z in range(0, Z, wide):
            stack = []
            for n in range(z, z + wide):
                stack.append(jnp.concatenate(
                    [r_ref[f, x + 1, n, wide_y, :] for f in range(F)]
                    + [q_ref[f, x, n, wide_y, :] for f in range(F)]
                    + [w_ref[f, x, n, y, :] for f in range(F)], axis=0))
            fields = jnp.concatenate(stack, axis=1)
            high = fields.astype(jnp.bfloat16)
            low = (fields - high.astype(jnp.float32)).astype(jnp.bfloat16)
            both = jnp.concatenate([high, low], axis=0)
            out = jnp.dot(coef[...], both, preferred_element_type=jnp.float32)
            n_out = 2 * F * TILE
            out = out[:n_out] + out[n_out:]
            at = pl.ds(z * LANES, wide * LANES)
            for j in range(F):
                x_ref[j, x, y, at] = out[j * TILE:(j + 1) * TILE]
                e_ref[j, x, y, at] = out[(F + j) * TILE:(F + j + 1) * TILE]

    def out_copies(x):
        return (
            pltpu.make_async_copy(x_ref.at[:, x], x_out.at[:, x], sems.at[0, x]),
            pltpu.make_async_copy(e_ref.at[:, x], e_out.at[:, x], sems.at[1, x]),
        )

    def plane(x, c):
        for t in range(cy // TILE):
            tile(x, t)
        for copy in out_copies(x):
            copy.start()
        return c

    def finish(x, c):
        for copy in out_copies(x):
            copy.wait()
        return c

    lax.fori_loop(0, cx, plane, 0)
    lax.fori_loop(0, cx, finish, 0)


def shards(nx, ny, adj, sig, elec):
    cx, cy, cz = sig.shape
    Z = cz // LANES
    current = math.sqrt(nx * cx * ny * cy * cz)
    block = jax.ShapeDtypeStruct(adj.shape, jnp.float32)
    hbm = pl.BlockSpec(memory_space=pltpu.HBM)
    vmem = pl.BlockSpec(memory_space=pltpu.VMEM)
    tall = cy + 2 * TILE
    f32 = lambda *dims: pltpu.VMEM(dims, jnp.float32)
    shape = lambda *dims: jax.ShapeDtypeStruct(dims, jnp.float32)
    dma = pltpu.SemaphoreType.DMA
    adj = pltpu.with_memory_space_constraint(adj, pltpu.HBM)
    sig = pltpu.with_memory_space_constraint(sig, pltpu.HBM)
    elec = pltpu.with_memory_space_constraint(elec, pltpu.HBM)
    slots = max(Z // 2, 1)
    r, q, w, sums = pl.pallas_call(
        functools.partial(operator_kernel, nx, ny, current),
        out_shape=(
            shape(F, cx + 2, Z, tall, LANES), shape(F, cx, Z, tall, LANES), shape(F, cx, Z, cy, LANES),
            shape(TILE, LANES),
        ),
        in_specs=[hbm, hbm, hbm],
        out_specs=(vmem, vmem, vmem, vmem),
        scratch_shapes=[
            pltpu.SMEM((F,), jnp.int32),
            f32(cx + 2, Z, tall, LANES),
            f32(7, cx, Z, cy, LANES),
            f32(2, F, Z, cy, LANES),
            f32(slots, F + 1, cy, LANES),
            f32(slots, F, cy, LANES),
            f32(4 * NP, TILE, LANES),
            f32(nx, TILE, LANES),
            f32(ny, TILE, LANES),
            dma((3,)), dma((2,)), dma((2, 2, Z)), dma((2, slots)), dma((1,)),
            dma((2,)), dma((2, 5)),
            dma((1,)), dma((1,)), dma((1,)), dma((1,)),
        ],
        compiler_params=pltpu.CompilerParams(collective_id=0, has_side_effects=True, vmem_limit_bytes=GRANT_A),
    )(adj, sig, elec)
    return pl.pallas_call(
        finish_kernel,
        out_shape=(block, block),
        in_specs=[vmem, vmem, vmem, vmem],
        out_specs=(hbm, hbm),
        scratch_shapes=[
            f32(F, cx, cy, cz), f32(F, cx, cy, cz),
            pltpu.VMEM((4 * F * TILE, 6 * F * TILE), jnp.bfloat16),
            dma((2, cx)),
        ],
        compiler_params=pltpu.CompilerParams(vmem_limit_bytes=GRANT_B),
    )(sums, r, q, w)


def solution(mesh):
    placed = (P(None, "gx", "gy", None), P("gx", "gy", None), P())
    return jax.shard_map(
        functools.partial(shards, mesh.shape["gx"], mesh.shape["gy"]),
        mesh=mesh,
        in_specs=placed,
        out_specs=(P(None, "gx", "gy", None), P(None, "gx", "gy", None)),
        check_vma=False,
    )
```

```python
import functools
import math

import jax
import jax.numpy as jnp
from jax import lax
from jax.experimental import pallas as pl
from jax.experimental.pallas import tpu as pltpu
from jax.sharding import PartitionSpec as P

MESH = pl.DeviceIdType.MESH
F = 4
PAIRS = [(i, j) for i in range(F) for j in range(i, F)]
NP = len(PAIRS)
TILE = 8
GRANT_A = 16 * 1024 * 1024
GRANT_B = 12 * 1024 * 1024
LANES = 128


def remote(src, dst, send, recv, axis, index):
    return pltpu.make_async_remote_copy(
        src_ref=src, dst_ref=dst, send_sem=send, recv_sem=recv,
        device_id={axis: index}, device_id_type=MESH,
    )


def operator_kernel(
    nx, ny, current, adj, sig, elec_ref, R, Q, W, sums,
    elec, S, wt, qx, relay_r, relay_q, acc, part_x, part_y,
    local, xs, xr, hr, fs, ys, yr, ax_s, ax_r, ay_s, ay_r,
):
    cx, cy, cz = sig.shape
    Z = cz // LANES
    T = cy // TILE
    total_y = ny * cy
    mx, my = lax.axis_index("gx"), lax.axis_index("gy")
    barrier = pltpu.get_barrier_semaphore()
    rows = pl.ds(TILE, cy)
    inner = pl.ds(1, cx)

    for axis, me, n in (("gx", mx, nx), ("gy", my, ny)):
        for d in range(1, n):
            pl.semaphore_signal(
                barrier, inc=1, device_id={axis: lax.rem(me + d, n)}, device_id_type=MESH
            )

    loads = [pltpu.make_async_copy(elec_ref, elec, local.at[2])]
    for z in range(Z):
        at = pl.ds(z * LANES, LANES)
        loads.append(pltpu.make_async_copy(adj.at[:, :, :, at], R.at[:, inner, z, rows, :], local.at[0]))
        loads.append(pltpu.make_async_copy(sig.at[:, :, at], S.at[inner, z, rows, :], local.at[1]))
    for load in loads:
        load.start()

    has_lo, has_hi = mx > 0, mx < nx - 1
    below, above = jnp.maximum(mx - 1, 0), jnp.minimum(mx + 1, nx - 1)
    y_lo, y_hi = my > 0, my < ny - 1
    left, right = jnp.maximum(my - 1, 0), jnp.minimum(my + 1, ny - 1)

    def take(ref, sem):
        pltpu.make_async_copy(ref, ref, sem).wait()

    half = Z // 2
    mid = nx // 2
    relaying = nx >= 4
    order = [z for k in range(half) for z in (k, Z - 1 - k)] + ([half] if Z % 2 else [])
    first_up = [z for k, z in enumerate(order) if k % 4 in (0, 3)]
    first_dn = [z for z in order if z not in first_up]
    relay_0 = order[Z - half:] if relaying else []
    relay_1 = order[:half] if relaying else []
    up_cross, dn_cross = mx == mid - 1, mx == mid
    up_end, dn_end = mx == nx - 1, mx == 0

    def lanes(z):
        return pl.ds(z * LANES, LANES)

    def hop(d, k, z, axis_to):
        plane = cx - 1 if d == 0 else 0
        halo = 0 if d == 0 else cx + 1
        if k == 0:
            pairs = [
                (adj.at[:, plane, :, lanes(z)], R.at[:, halo, z, rows, :]),
                (sig.at[plane, :, lanes(z)], S.at[halo, z, rows, :]),
            ]
        else:
            pairs = [(Q.at[:, plane, z, rows, :], qx.at[d, :, z])]
        return [remote(src, dst, xs.at[d, k], xr.at[d, k, z], "gx", axis_to) for src, dst in pairs]

    def to_relay(d, k, z):
        plane = cx - 1 if d == 0 else 0
        end = nx - 1 if d == 0 else 0
        if k == 0:
            at = relay_0.index(z)
            pairs = [
                (adj.at[:, plane, :, lanes(z)], relay_r.at[at, pl.ds(0, F)]),
                (sig.at[plane, :, lanes(z)], relay_r.at[at, F]),
            ]
        else:
            at = relay_1.index(z)
            pairs = [(Q.at[:, plane, z, rows, :], relay_q.at[at])]
        return [remote(src, dst, xs.at[d, k], hr.at[k, at], "gx", end) for src, dst in pairs]

    def from_relay(d, k, z):
        halo = 0 if d == 0 else cx + 1
        target = mid if d == 0 else mid - 1
        if k == 0:
            at = relay_0.index(z)
            pairs = [
                (relay_r.at[at, pl.ds(0, F)], R.at[:, halo, z, rows, :]),
                (relay_r.at[at, F], S.at[halo, z, rows, :]),
            ]
        else:
            pairs = [(relay_q.at[relay_1.index(z)], qx.at[d, :, z])]
        return [remote(src, dst, fs.at[k], xr.at[d, k, z], "gx", target) for src, dst in pairs]

    sides = ((0, has_hi, above, up_cross, up_end), (1, has_lo, below, dn_cross, dn_end))

    def start(copies):
        for copy in copies:
            copy.start()

    def send_relayed(d, k, z):
        if z in (relay_0, relay_1)[k]:
            @pl.when(sides[d][3])
            def _():
                start(to_relay(d, k, z))

    def send_direct(d, k, z):
        _, there, to, cross, _ = sides[d]
        if z in (relay_0, relay_1)[k]:
            there = there & jnp.logical_not(cross)

        @pl.when(there)
        def _():
            start(hop(d, k, z, to))

    def forward(d, k, z):
        if z in (relay_0, relay_1)[k]:
            @pl.when(sides[d][4])
            def _():
                at = (relay_0, relay_1)[k].index(z)
                take((relay_r, relay_q)[k].at[at], hr.at[k, at])
                start(from_relay(d, k, z))

    def arrive(d, k, z):
        take((relay_r, relay_q)[k].at[0], xr.at[d, k, z])

    def y_hop(d, k):
        src_row, dst_row = (TILE + cy - 1, TILE - 1) if d == 0 else (TILE, TILE + cy)
        to = right if d == 0 else left
        if k == 0:
            src, dst = R.at[:, inner, :, src_row, :], R.at[:, inner, :, dst_row, :]
        elif k == 1:
            src, dst = S.at[inner, :, src_row, :], S.at[inner, :, dst_row, :]
        elif k == 2:
            span = pl.ds(1, cx - 2)
            src, dst = Q.at[:, span, :, src_row, :], Q.at[:, span, :, dst_row, :]
        else:
            x = 0 if k == 3 else cx - 1
            src, dst = Q.at[:, x, :, src_row, :], Q.at[:, x, :, dst_row, :]
        return remote(src, dst, ys.at[d], yr.at[d, k], "gy", to)

    def y_send(kinds):
        for d, there in ((0, y_hi), (1, y_lo)):
            @pl.when(there)
            def _():
                for k in kinds:
                    y_hop(d, k).start()

    def y_arrive(kinds):
        for d, there in ((0, y_lo), (1, y_hi)):
            @pl.when(there)
            def _():
                for k in kinds:
                    y_hop(d, k).wait_recv()

    pl.semaphore_wait(barrier, nx + ny - 2)
    for z in order:
        for d in (0, 1):
            send_relayed(d, 0, z)
    for z in order:
        for d in (0, 1):
            send_direct(d, 0, z)

    acc[...] = jnp.zeros_like(acc)
    nothing = jnp.zeros((cy, LANES), jnp.float32)
    no_row = jnp.zeros((1, LANES), jnp.float32)
    take(W, local.at[0])
    take(wt.at[0], local.at[1])
    loads[0].wait()

    row_id = lax.broadcasted_iota(jnp.int32, (cy, LANES), 0)
    first = lax.broadcasted_iota(jnp.int32, (cy, LANES), 1) == 0

    def spike(x):
        cell = row_id + ((mx * cx + x - 1) * total_y + my * cy)
        for f in range(F):
            here = jnp.where(first & (cell == elec[f]), current, 0.0)
            R[f, x, 0, rows, :] = R[f, x, 0, rows, :] + here

    def loop(lo, hi, body):
        def one(k, c):
            body(k)
            return c
        lax.fori_loop(lo, hi, one, 0)

    loop(1, cx + 1, spike)
    y_send((0, 1))

    for there, halo, own in ((has_lo, 0, 1), (has_hi, cx + 1, cx)):
        @pl.when(jnp.logical_not(there))
        def _():
            for z in range(Z):
                S[halo, z, rows, :] = S[own, z, rows, :]
                for f in range(F):
                    R[f, halo, z, rows, :] = nothing

    for there, halo, own in ((y_lo, TILE - 1, TILE), (y_hi, TILE + cy, TILE + cy - 1)):
        @pl.when(jnp.logical_not(there))
        def _():
            def fill(x):
                for z in range(Z):
                    S[x + 1, z, pl.ds(halo, 1), :] = S[x + 1, z, pl.ds(own, 1), :]
                    for f in range(F):
                        R[f, x + 1, z, pl.ds(halo, 1), :] = no_row
                        Q[f, x, z, pl.ds(halo, 1), :] = no_row
            loop(0, cx, fill)

    lane = lax.broadcasted_iota(jnp.int32, (TILE, LANES), 1)
    lane_lo, lane_hi = lane == 0, lane == LANES - 1

    def beside(get, zs, edge):
        blocks, fwd, bwd = {}, {}, {}
        for z in zs:
            for n in (z - 1, z, z + 1):
                if 0 <= n < Z and n not in blocks:
                    blocks[n] = get(n)
        for z in zs:
            for n in (z - 1, z):
                if n in blocks and n not in fwd:
                    fwd[n] = pltpu.roll(blocks[n], 1, axis=1)
            for n in (z, z + 1):
                if n in blocks and n not in bwd:
                    bwd[n] = pltpu.roll(blocks[n], LANES - 1, axis=1)
        out = {}
        for z in zs:
            before = fwd[z - 1] if z > 0 else edge(blocks[z])
            after = bwd[z + 1] if z < Z - 1 else edge(blocks[z])
            out[z] = (
                blocks[z],
                jnp.where(lane_lo, before, fwd[z]),
                jnp.where(lane_hi, after, bwd[z]),
            )
        return out

    def add_grams(base, lefts, rights):
        zs = list(lefts[0])
        for k, (i, j) in enumerate(PAIRS):
            total = None
            for z in zs:
                prod = lefts[i][z] * rights[j][z]
                total = prod if total is None else total + prod
            acc[base + k] = acc[base + k] + total

    def first_tile(x, t, zs):
        y = t * TILE
        at, up, dn = pl.ds(y + TILE, TILE), pl.ds(y + TILE - 1, TILE), pl.ds(y + TILE + 1, TILE)
        out_at = pl.ds(y, TILE)
        weights = {}
        near = beside(lambda z: S[x, z, at, :], zs, lambda v: v)
        for z in zs:
            here, zm, zp = near[z]
            faces = [
                here + S[x - 1, z, at, :], here + S[x + 1, z, at, :],
                here + S[x, z, up, :], here + S[x, z, dn, :], here + zm, here + zp,
            ]
            diag = ((faces[0] + faces[1]) + (faces[2] + faces[3])) + (faces[4] + faces[5])
            weights[z] = [diag] + faces
            for k in range(7):
                wt[k, x - 1, z, out_at, :] = weights[z][k]
        rs, qs = [], []
        for f in range(F):
            near = beside(lambda z: R[f, x, z, at, :], zs, jnp.zeros_like)
            r, q = {}, {}
            for z in zs:
                mid_v, zm, zp = near[z]
                d, wxm, wxp, wym, wyp, wzm, wzp = weights[z]
                out = d * mid_v - wzm * zm - wzp * zp
                out = out - wxm * R[f, x - 1, z, at, :] - wxp * R[f, x + 1, z, at, :]
                out = out - wym * R[f, x, z, up, :] - wyp * R[f, x, z, dn, :]
                Q[f, x - 1, z, at, :] = out
                r[z], q[z] = mid_v, out
            rs.append(r)
            qs.append(q)
        add_grams(0, rs, rs)
        add_grams(NP, rs, qs)

    def second_tile(x, t, zs, low, high):
        y = t * TILE
        at, up, dn = pl.ds(y + TILE, TILE), pl.ds(y + TILE - 1, TILE), pl.ds(y + TILE + 1, TILE)
        out_at = pl.ds(y, TILE)
        qs, ws = [], []
        for f in range(F):
            near = beside(lambda z: Q[f, x - 1, z, at, :], zs, jnp.zeros_like)
            q, w = {}, {}
            for z in zs:
                mid_v, zm, zp = near[z]
                out = wt[0, x - 1, z, out_at, :] * mid_v
                out = out - wt[5, x - 1, z, out_at, :] * zm - wt[6, x - 1, z, out_at, :] * zp
                if low:
                    out = out - wt[1, x - 1, z, out_at, :] * Q[f, x - 2, z, at, :]
                if high:
                    out = out - wt[2, x - 1, z, out_at, :] * Q[f, x, z, at, :]
                out = out - wt[3, x - 1, z, out_at, :] * Q[f, x - 1, z, up, :]
                out = out - wt[4, x - 1, z, out_at, :] * Q[f, x - 1, z, dn, :]
                W[f, x - 1, z, out_at, :] = out
                q[z], w[z] = mid_v, out
            qs.append(q)
            ws.append(w)
        add_grams(2 * NP, qs, qs)
        add_grams(3 * NP, qs, ws)

    def face_tile(d, z, t, grams):
        x = 0 if d == 0 else cx - 1
        y = pl.multiple_of(t * TILE, TILE)
        at, out_at = pl.ds(y + TILE, TILE), pl.ds(y, TILE)
        face = wt[1 + d, x, z, out_at, :]
        vs = [face * qx[d, f, z, out_at, :] for f in range(F)]
        for f in range(F):
            W[f, x, z, out_at, :] = W[f, x, z, out_at, :] - vs[f]
        if grams:
            qs = [Q[f, x, z, at, :] for f in range(F)]
            for k, (i, j) in enumerate(PAIRS):
                acc[3 * NP + k] = acc[3 * NP + k] - (qs[i] * vs[j] + vs[i] * qs[j])

    def face(d, z, grams):
        @pl.when((has_lo, has_hi)[d])
        def _():
            arrive(d, 1, z)
            loop(0, T, lambda t: face_tile(d, z, t, grams))

    every = list(range(Z))

    def middle(planes, tile, *rest):
        lo, hi = planes
        def plane(x):
            for t in range(1, T - 1):
                tile(x, t, every, *rest)
        loop(lo, hi, plane)

    def rims(planes, tile, *rest):
        lo, hi = planes
        def plane(x):
            for t in (0, T - 1):
                tile(x, t, every, *rest)
        loop(lo, hi, plane)

    def chunk(z):
        for d, there in ((0, has_lo), (1, has_hi)):
            @pl.when(there)
            def _():
                arrive(d, 0, z)
        if z == 0:
            loop(0, 2, lambda k: spike(k * (cx + 1)))
        def plane(k):
            for t in range(T):
                first_tile(1 + k * (cx - 1), t, [z])
        loop(0, 2, plane)

    def forward_all(k, zs, ds=(0, 1)):
        for z in zs:
            for d in ds:
                forward(d, k, z)

    firsts = (first_up, first_dn)
    late = [(d, z) for z in order for d in (0, 1) if z not in firsts[d]]
    early = [(d, z) for z in order for d in (0, 1) if z in firsts[d]]
    split = (cx + 2) // 2
    middle((2, split), first_tile)
    middle((split, cx), first_tile)
    y_arrive((0, 1))
    forward_all(0, relay_0[:1])
    rims((2, cx), first_tile)
    y_send((2,))
    forward_all(0, relay_0[1:])
    middle((3, cx - 1), second_tile, True, True)
    for n, z in enumerate(order):
        if n == 2:
            y_arrive((2,))
            rims((3, cx - 1), second_tile, True, True)
        if n == Z - 1:
            for d in (0, 1):
                @pl.when(sides[d][1])
                def _():
                    take(wt.at[0, pl.ds(0, F + 1)], xs.at[d, 0])
                for c in order[:n]:
                    if c in firsts[d]:
                        send_direct(d, 1, c)
        chunk(z)
        for d in (0, 1):
            send_relayed(d, 1, z)
    for d in (0, 1):
        if order[Z - 1] in firsts[d]:
            send_direct(d, 1, order[Z - 1])
    for d, c in late[:half]:
        send_direct(d, 1, c)
    y_send((3, 4))

    def beside_ends(k):
        for t in range(T):
            second_tile(2 + k * (cx - 3), t, every, True, True)
    loop(0, 2, beside_ends)
    for d, z in early:
        forward(d, 1, z)
    middle((1, 2), second_tile, False, True)
    middle((cx, cx + 1), second_tile, True, False)
    y_arrive((3, 4))
    rims((1, 2), second_tile, False, True)
    rims((cx, cx + 1), second_tile, True, False)
    for d, z in late[:half]:
        forward(d, 1, z)
    for d, z in early:
        face(d, z, True)

    def compact(parts):
        lane_sum = jnp.sum(parts, axis=1, keepdims=True)
        out = jnp.zeros((TILE, LANES), jnp.float32)
        for k in range(4 * NP // TILE):
            out = jnp.where(lane == k, lane_sum[k * TILE:(k + 1) * TILE], out)
        return out

    part_x[mx] = compact(jnp.sum(acc[...], axis=1))

    def exchange(buf, axis, me, n, sends, recvs):
        for d in range(1, n):
            remote(buf.at[me], buf.at[me], sends.at[0], recvs.at[0], axis, lax.rem(me + d, n)).start()

    def gather(buf, n, recvs):
        if n > 1:
            take(buf.at[pl.ds(0, n - 1)], recvs.at[0])
        total = buf[0]
        for k in range(1, n):
            total = total + buf[k]
        return total

    exchange(part_x, "gx", mx, nx, ax_s, ax_r)
    for d, z in late[half:]:
        send_direct(d, 1, z)
    part_y[my] = gather(part_x, nx, ax_r)
    exchange(part_y, "gy", my, ny, ay_s, ay_r)
    for d, z in late[half:]:
        forward(d, 1, z)
    for d, z in late:
        face(d, z, False)
    sums[...] = gather(part_y, ny, ay_r)

    if nx > 1:
        take(part_x.at[pl.ds(0, nx - 1)], ax_s.at[0])
    if ny > 1:
        take(part_y.at[pl.ds(0, ny - 1)], ay_s.at[0])
    for d in (0, 1):
        @pl.when(sides[d][1])
        def _():
            take(W.at[0, pl.ds(0, F)], xs.at[d, 1])

        @pl.when((y_hi, y_lo)[d])
        def _():
            take(wt.at[0, :, :, pl.ds(0, 2 * F + 1), :], ys.at[d])

    if relay_0 and relay_1:
        @pl.when(up_end | dn_end)
        def _():
            take(relay_r.at[pl.ds(0, len(relay_0))], fs.at[0])
            take(relay_q.at[pl.ds(0, len(relay_1))], fs.at[1])


def mat(a, b):
    return [
        [sum(a[i][k] * b[k][j] for k in range(1, F)) + a[i][0] * b[0][j] for j in range(F)]
        for i in range(F)
    ]


def add(a, b):
    return [[a[i][j] + b[i][j] for j in range(F)] for i in range(F)]


def sub(a, b):
    return [[a[i][j] - b[i][j] for j in range(F)] for i in range(F)]


def turn(a):
    return [[a[j][i] for j in range(F)] for i in range(F)]


def spd_solve(a, b):
    low = [[None] * F for _ in range(F)]
    inv = [None] * F
    rest = [list(row) for row in a]
    for k in range(F):
        inv[k] = 1.0 / rest[k][k]
        for i in range(k + 1, F):
            low[i][k] = rest[i][k] * inv[k]
        for i in range(k + 1, F):
            for j in range(k + 1, i + 1):
                rest[i][j] = rest[i][j] - low[i][k] * rest[j][k]
    out = [list(row) for row in b]
    for i in range(F):
        for k in range(i):
            out[i] = [u - low[i][k] * v for u, v in zip(out[i], out[k])]
    out = [[u * inv[i] for u in out[i]] for i in range(F)]
    for i in reversed(range(F)):
        for k in range(i + 1, F):
            out[i] = [u - low[k][i] * v for u, v in zip(out[i], out[k])]
    return out


def finish_kernel(sums, r_ref, q_ref, w_ref, x_out, e_out, x_ref, e_ref, coef, sems):
    def prepare():
        lane = lax.broadcasted_iota(jnp.int32, (TILE, LANES), 1)
        rows = []
        for k in range(4 * NP // TILE):
            column = jnp.sum(jnp.where(lane == k, sums[...], 0.0), axis=1, keepdims=True)
            wide = jnp.broadcast_to(column, (TILE, LANES))
            rows.extend(wide[s:s + 1] for s in range(TILE))
        grams = []
        for g in range(4):
            m = [[None] * F for _ in range(F)]
            for k, (i, j) in enumerate(PAIRS):
                m[i][j] = m[j][i] = rows[g * NP + k]
            grams.append(m)
        s0, s1, s2, s3 = grams
        a0 = spd_solve(s1, s0)
        s1a, s2a = mat(s1, a0), mat(s2, a0)
        a0t = turn(a0)
        rr = add(sub(sub(s0, s1a), turn(s1a)), mat(a0t, s2a))
        cross = add(sub(sub(s1, s2a), turn(s2a)), mat(a0t, mat(s3, a0)))
        beta = spd_solve(s0, rr)
        curve = sub(cross, mat(turn(beta), mat(s1, beta)))
        a1 = spd_solve(curve, rr)
        m1 = add(add(a0, a1), mat(beta, a1))
        m2 = mat(a0, a1)
        zero = jnp.zeros_like(m1[0][0])
        one = zero + 1.0
        weights = []
        for j in range(F):
            weights.append([m1[i][j] + m1[i][j] for i in range(F)] + [-(m2[i][j] + m2[i][j]) for i in range(F)] + [zero] * F)
        for j in range(F):
            unit = [one if i == j else zero for i in range(F)]
            weights.append(unit + [-m1[i][j] for i in range(F)] + [m2[i][j] for i in range(F)])
        depth = 3 * F * TILE
        row_s = lax.broadcasted_iota(jnp.int32, (TILE, LANES), 0)
        blocks = [[None] * 2 for _ in weights]
        for h in range(2):
            column = lane + h * LANES
            column = jnp.where(column >= depth, column - depth, column)
            at = [column == k * TILE + row_s for k in range(3 * F)]
            for j, row in enumerate(weights):
                block = jnp.zeros((TILE, LANES), jnp.float32)
                for k in range(3 * F):
                    if row[k] is not zero:
                        block = jnp.where(at[k], jnp.broadcast_to(row[k], block.shape), block)
                blocks[j][h] = block
        full = jnp.concatenate([jnp.concatenate(pair, axis=1) for pair in blocks], axis=0)[:, :2 * depth]
        high = full.astype(jnp.bfloat16)
        low = (full - high.astype(jnp.float32)).astype(jnp.bfloat16)
        coef[...] = jnp.concatenate([high, low], axis=0)

    prepare()
    cx, Z, cy = w_ref.shape[1:4]
    wide = 2 if Z % 2 == 0 else 1

    def tile(x, t):
        y, wide_y = pl.ds(t * TILE, TILE), pl.ds(t * TILE + TILE, TILE)
        for z in range(0, Z, wide):
            stack = []
            for n in range(z, z + wide):
                stack.append(jnp.concatenate(
                    [r_ref[f, x + 1, n, wide_y, :] for f in range(F)]
                    + [q_ref[f, x, n, wide_y, :] for f in range(F)]
                    + [w_ref[f, x, n, y, :] for f in range(F)], axis=0))
            fields = jnp.concatenate(stack, axis=1)
            high = fields.astype(jnp.bfloat16)
            low = (fields - high.astype(jnp.float32)).astype(jnp.bfloat16)
            both = jnp.concatenate([high, low], axis=0)
            out = jnp.dot(coef[...], both, preferred_element_type=jnp.float32)
            n_out = 2 * F * TILE
            out = out[:n_out] + out[n_out:]
            at = pl.ds(z * LANES, wide * LANES)
            for j in range(F):
                x_ref[j, x, y, at] = out[j * TILE:(j + 1) * TILE]
                e_ref[j, x, y, at] = out[(F + j) * TILE:(F + j + 1) * TILE]

    parts = 2 if cy % (2 * TILE) == 0 else 1
    part = cy // parts

    def out_copies(x, h):
        y = pl.ds(h * part, part)
        return (
            pltpu.make_async_copy(x_ref.at[:, x, y], x_out.at[:, x, y], sems.at[0, x, h]),
            pltpu.make_async_copy(e_ref.at[:, x, y], e_out.at[:, x, y], sems.at[1, x, h]),
        )

    def plane(x, c):
        for h in range(parts):
            for t in range(h * part // TILE, (h + 1) * part // TILE):
                tile(x, t)
            for copy in out_copies(x, h):
                copy.start()
        return c

    lax.fori_loop(0, cx, plane, 0)
    for x in range(cx):
        for h in range(parts):
            for copy in out_copies(x, h):
                copy.wait()


def shards(nx, ny, adj, sig, elec):
    cx, cy, cz = sig.shape
    Z = cz // LANES
    current = math.sqrt(nx * cx * ny * cy * cz)
    block = jax.ShapeDtypeStruct(adj.shape, jnp.float32)
    hbm = pl.BlockSpec(memory_space=pltpu.HBM)
    vmem = pl.BlockSpec(memory_space=pltpu.VMEM)
    tall = cy + 2 * TILE
    f32 = lambda *dims: pltpu.VMEM(dims, jnp.float32)
    shape = lambda *dims: jax.ShapeDtypeStruct(dims, jnp.float32)
    dma = pltpu.SemaphoreType.DMA
    adj = pltpu.with_memory_space_constraint(adj, pltpu.HBM)
    sig = pltpu.with_memory_space_constraint(sig, pltpu.HBM)
    elec = pltpu.with_memory_space_constraint(elec, pltpu.HBM)
    slots = max(Z // 2, 1)
    r, q, w, sums = pl.pallas_call(
        functools.partial(operator_kernel, nx, ny, current),
        out_shape=(
            shape(F, cx + 2, Z, tall, LANES), shape(F, cx, Z, tall, LANES), shape(F, cx, Z, cy, LANES),
            shape(TILE, LANES),
        ),
        in_specs=[hbm, hbm, hbm],
        out_specs=(vmem, vmem, vmem, vmem),
        scratch_shapes=[
            pltpu.SMEM((F,), jnp.int32),
            f32(cx + 2, Z, tall, LANES),
            f32(7, cx, Z, cy, LANES),
            f32(2, F, Z, cy, LANES),
            f32(slots, F + 1, cy, LANES),
            f32(slots, F, cy, LANES),
            f32(4 * NP, TILE, LANES),
            f32(nx, TILE, LANES),
            f32(ny, TILE, LANES),
            dma((3,)), dma((2, 2)), dma((2, 2, Z)), dma((2, slots)), dma((2,)),
            dma((2,)), dma((2, 5)),
            dma((1,)), dma((1,)), dma((1,)), dma((1,)),
        ],
        compiler_params=pltpu.CompilerParams(collective_id=0, has_side_effects=True, vmem_limit_bytes=GRANT_A),
    )(adj, sig, elec)
    return pl.pallas_call(
        finish_kernel,
        out_shape=(block, block),
        in_specs=[vmem, vmem, vmem, vmem],
        out_specs=(hbm, hbm),
        scratch_shapes=[
            f32(F, cx, cy, cz), f32(F, cx, cy, cz),
            pltpu.VMEM((4 * F * TILE, 6 * F * TILE), jnp.bfloat16),
            dma((2, cx, 2)),
        ],
        compiler_params=pltpu.CompilerParams(vmem_limit_bytes=GRANT_B),
    )(sums, r, q, w)


def solution(mesh):
    placed = (P(None, "gx", "gy", None), P("gx", "gy", None), P())
    return jax.shard_map(
        functools.partial(shards, mesh.shape["gx"], mesh.shape["gy"]),
        mesh=mesh,
        in_specs=placed,
        out_specs=(P(None, "gx", "gy", None), P(None, "gx", "gy", None)),
        check_vma=False,
    )
```

```python
import functools
import math

import jax
import jax.numpy as jnp
from jax import lax
from jax.experimental import pallas as pl
from jax.experimental.pallas import tpu as pltpu
from jax.sharding import PartitionSpec as P

MESH = pl.DeviceIdType.MESH
F = 4
PAIRS = [(i, j) for i in range(F) for j in range(i, F)]
NP = len(PAIRS)
TILE = 8
GRANT_A = 16 * 1024 * 1024
GRANT_B = 12 * 1024 * 1024
LANES = 128


def remote(src, dst, send, recv, axis, index):
    return pltpu.make_async_remote_copy(
        src_ref=src, dst_ref=dst, send_sem=send, recv_sem=recv,
        device_id={axis: index}, device_id_type=MESH,
    )


def operator_kernel(
    nx, ny, current, adj, sig, elec_ref, R, Q, W, sums,
    elec, S, wt, qx, relay_r, relay_q, acc, part_x, part_y,
    local, xs, xr, hr, fs, ys, yr, ax_s, ax_r, ay_s, ay_r,
):
    cx, cy, cz = sig.shape
    Z = cz // LANES
    T = cy // TILE
    total_y = ny * cy
    mx, my = lax.axis_index("gx"), lax.axis_index("gy")
    barrier = pltpu.get_barrier_semaphore()
    rows = pl.ds(TILE, cy)
    inner = pl.ds(1, cx)

    for axis, me, n in (("gx", mx, nx), ("gy", my, ny)):
        for d in range(1, n):
            pl.semaphore_signal(
                barrier, inc=1, device_id={axis: lax.rem(me + d, n)}, device_id_type=MESH
            )

    loads = [pltpu.make_async_copy(elec_ref, elec, local.at[2])]
    for z in range(Z):
        at = pl.ds(z * LANES, LANES)
        loads.append(pltpu.make_async_copy(adj.at[:, :, :, at], R.at[:, inner, z, rows, :], local.at[0]))
        loads.append(pltpu.make_async_copy(sig.at[:, :, at], S.at[inner, z, rows, :], local.at[1]))
    for load in loads:
        load.start()

    has_lo, has_hi = mx > 0, mx < nx - 1
    below, above = jnp.maximum(mx - 1, 0), jnp.minimum(mx + 1, nx - 1)
    y_lo, y_hi = my > 0, my < ny - 1
    left, right = jnp.maximum(my - 1, 0), jnp.minimum(my + 1, ny - 1)

    def take(ref, sem):
        pltpu.make_async_copy(ref, ref, sem).wait()

    half = Z // 2
    mid = nx // 2
    relaying = nx >= 4
    order = [z for k in range(half) for z in (k, Z - 1 - k)] + ([half] if Z % 2 else [])
    first_up = [z for k, z in enumerate(order) if k % 4 in (0, 3)]
    first_dn = [z for z in order if z not in first_up]
    relay_0 = order[1::2] if relaying else []
    relay_1 = order[:half] if relaying else []
    up_cross, dn_cross = mx == mid - 1, mx == mid
    up_end, dn_end = mx == nx - 1, mx == 0

    def lanes(z):
        return pl.ds(z * LANES, LANES)

    def hop(d, k, z, axis_to):
        plane = cx - 1 if d == 0 else 0
        halo = 0 if d == 0 else cx + 1
        if k == 0:
            pairs = [
                (adj.at[:, plane, :, lanes(z)], R.at[:, halo, z, rows, :]),
                (sig.at[plane, :, lanes(z)], S.at[halo, z, rows, :]),
            ]
        else:
            pairs = [(Q.at[:, plane, z, rows, :], qx.at[d, :, z])]
        return [remote(src, dst, xs.at[d, k], xr.at[d, k, z], "gx", axis_to) for src, dst in pairs]

    def to_relay(d, k, z):
        plane = cx - 1 if d == 0 else 0
        end = nx - 1 if d == 0 else 0
        if k == 0:
            at = relay_0.index(z)
            pairs = [
                (adj.at[:, plane, :, lanes(z)], relay_r.at[at, pl.ds(0, F)]),
                (sig.at[plane, :, lanes(z)], relay_r.at[at, F]),
            ]
        else:
            at = relay_1.index(z)
            pairs = [(Q.at[:, plane, z, rows, :], relay_q.at[at])]
        return [remote(src, dst, xs.at[d, k], hr.at[k, at], "gx", end) for src, dst in pairs]

    def from_relay(d, k, z):
        halo = 0 if d == 0 else cx + 1
        target = mid if d == 0 else mid - 1
        if k == 0:
            at = relay_0.index(z)
            pairs = [
                (relay_r.at[at, pl.ds(0, F)], R.at[:, halo, z, rows, :]),
                (relay_r.at[at, F], S.at[halo, z, rows, :]),
            ]
        else:
            pairs = [(relay_q.at[relay_1.index(z)], qx.at[d, :, z])]
        return [remote(src, dst, fs.at[k], xr.at[d, k, z], "gx", target) for src, dst in pairs]

    sides = ((0, has_hi, above, up_cross, up_end), (1, has_lo, below, dn_cross, dn_end))

    def start(copies):
        for copy in copies:
            copy.start()

    def send_relayed(d, k, z):
        if z in (relay_0, relay_1)[k]:
            @pl.when(sides[d][3])
            def _():
                start(to_relay(d, k, z))

    def send_direct(d, k, z):
        _, there, to, cross, _ = sides[d]
        if z in (relay_0, relay_1)[k]:
            there = there & jnp.logical_not(cross)

        @pl.when(there)
        def _():
            start(hop(d, k, z, to))

    def forward(d, k, z):
        if z in (relay_0, relay_1)[k]:
            @pl.when(sides[d][4])
            def _():
                at = (relay_0, relay_1)[k].index(z)
                take((relay_r, relay_q)[k].at[at], hr.at[k, at])
                start(from_relay(d, k, z))

    def arrive(d, k, z):
        take((relay_r, relay_q)[k].at[0], xr.at[d, k, z])

    def y_hop(d, k):
        src_row, dst_row = (TILE + cy - 1, TILE - 1) if d == 0 else (TILE, TILE + cy)
        to = right if d == 0 else left
        if k == 0:
            src, dst = R.at[:, inner, :, src_row, :], R.at[:, inner, :, dst_row, :]
        elif k == 1:
            src, dst = S.at[inner, :, src_row, :], S.at[inner, :, dst_row, :]
        elif k == 2:
            span = pl.ds(1, cx - 2)
            src, dst = Q.at[:, span, :, src_row, :], Q.at[:, span, :, dst_row, :]
        else:
            x = 0 if k == 3 else cx - 1
            src, dst = Q.at[:, x, :, src_row, :], Q.at[:, x, :, dst_row, :]
        return remote(src, dst, ys.at[d], yr.at[d, k], "gy", to)

    def y_send(kinds):
        for d, there in ((0, y_hi), (1, y_lo)):
            @pl.when(there)
            def _():
                for k in kinds:
                    y_hop(d, k).start()

    def y_arrive(kinds):
        for d, there in ((0, y_lo), (1, y_hi)):
            @pl.when(there)
            def _():
                for k in kinds:
                    y_hop(d, k).wait_recv()

    pl.semaphore_wait(barrier, nx + ny - 2)
    for z in order:
        for d in (0, 1):
            send_relayed(d, 0, z)
    for z in order:
        for d in (0, 1):
            send_direct(d, 0, z)

    acc[...] = jnp.zeros_like(acc)
    nothing = jnp.zeros((cy, LANES), jnp.float32)
    no_row = jnp.zeros((1, LANES), jnp.float32)
    take(W, local.at[0])
    take(wt.at[0], local.at[1])
    loads[0].wait()

    row_id = lax.broadcasted_iota(jnp.int32, (cy, LANES), 0)
    first = lax.broadcasted_iota(jnp.int32, (cy, LANES), 1) == 0

    def spike(x):
        cell = row_id + ((mx * cx + x - 1) * total_y + my * cy)
        for f in range(F):
            here = jnp.where(first & (cell == elec[f]), current, 0.0)
            R[f, x, 0, rows, :] = R[f, x, 0, rows, :] + here

    def loop(lo, hi, body):
        def one(k, c):
            body(k)
            return c
        lax.fori_loop(lo, hi, one, 0)

    loop(1, cx + 1, spike)
    y_send((0, 1))

    for there, halo, own in ((has_lo, 0, 1), (has_hi, cx + 1, cx)):
        @pl.when(jnp.logical_not(there))
        def _():
            for z in range(Z):
                S[halo, z, rows, :] = S[own, z, rows, :]
                for f in range(F):
                    R[f, halo, z, rows, :] = nothing

    for there, halo, own in ((y_lo, TILE - 1, TILE), (y_hi, TILE + cy, TILE + cy - 1)):
        @pl.when(jnp.logical_not(there))
        def _():
            def fill(x):
                for z in range(Z):
                    S[x + 1, z, pl.ds(halo, 1), :] = S[x + 1, z, pl.ds(own, 1), :]
                    for f in range(F):
                        R[f, x + 1, z, pl.ds(halo, 1), :] = no_row
                        Q[f, x, z, pl.ds(halo, 1), :] = no_row
            loop(0, cx, fill)

    lane = lax.broadcasted_iota(jnp.int32, (TILE, LANES), 1)
    lane_lo, lane_hi = lane == 0, lane == LANES - 1

    def beside(get, zs, edge):
        blocks, fwd, bwd = {}, {}, {}
        for z in zs:
            for n in (z - 1, z, z + 1):
                if 0 <= n < Z and n not in blocks:
                    blocks[n] = get(n)
        for z in zs:
            for n in (z - 1, z):
                if n in blocks and n not in fwd:
                    fwd[n] = pltpu.roll(blocks[n], 1, axis=1)
            for n in (z, z + 1):
                if n in blocks and n not in bwd:
                    bwd[n] = pltpu.roll(blocks[n], LANES - 1, axis=1)
        out = {}
        for z in zs:
            before = fwd[z - 1] if z > 0 else edge(blocks[z])
            after = bwd[z + 1] if z < Z - 1 else edge(blocks[z])
            out[z] = (
                blocks[z],
                jnp.where(lane_lo, before, fwd[z]),
                jnp.where(lane_hi, after, bwd[z]),
            )
        return out

    def add_grams(base, lefts, rights):
        zs = list(lefts[0])
        for k, (i, j) in enumerate(PAIRS):
            total = None
            for z in zs:
                prod = lefts[i][z] * rights[j][z]
                total = prod if total is None else total + prod
            acc[base + k] = acc[base + k] + total

    def first_tile(x, t, zs):
        y = t * TILE
        at, up, dn = pl.ds(y + TILE, TILE), pl.ds(y + TILE - 1, TILE), pl.ds(y + TILE + 1, TILE)
        out_at = pl.ds(y, TILE)
        weights = {}
        near = beside(lambda z: S[x, z, at, :], zs, lambda v: v)
        for z in zs:
            here, zm, zp = near[z]
            faces = [
                here + S[x - 1, z, at, :], here + S[x + 1, z, at, :],
                here + S[x, z, up, :], here + S[x, z, dn, :], here + zm, here + zp,
            ]
            diag = ((faces[0] + faces[1]) + (faces[2] + faces[3])) + (faces[4] + faces[5])
            weights[z] = [diag] + faces
            for k in range(7):
                wt[k, x - 1, z, out_at, :] = weights[z][k]
        rs, qs = [], []
        for f in range(F):
            near = beside(lambda z: R[f, x, z, at, :], zs, jnp.zeros_like)
            r, q = {}, {}
            for z in zs:
                mid_v, zm, zp = near[z]
                d, wxm, wxp, wym, wyp, wzm, wzp = weights[z]
                out = d * mid_v - wzm * zm - wzp * zp
                out = out - wxm * R[f, x - 1, z, at, :] - wxp * R[f, x + 1, z, at, :]
                out = out - wym * R[f, x, z, up, :] - wyp * R[f, x, z, dn, :]
                Q[f, x - 1, z, at, :] = out
                r[z], q[z] = mid_v, out
            rs.append(r)
            qs.append(q)
        add_grams(0, rs, rs)
        add_grams(NP, rs, qs)

    def second_tile(x, t, zs, low, high):
        y = t * TILE
        at, up, dn = pl.ds(y + TILE, TILE), pl.ds(y + TILE - 1, TILE), pl.ds(y + TILE + 1, TILE)
        out_at = pl.ds(y, TILE)
        qs, ws = [], []
        for f in range(F):
            near = beside(lambda z: Q[f, x - 1, z, at, :], zs, jnp.zeros_like)
            q, w = {}, {}
            for z in zs:
                mid_v, zm, zp = near[z]
                out = wt[0, x - 1, z, out_at, :] * mid_v
                out = out - wt[5, x - 1, z, out_at, :] * zm - wt[6, x - 1, z, out_at, :] * zp
                if low:
                    out = out - wt[1, x - 1, z, out_at, :] * Q[f, x - 2, z, at, :]
                if high:
                    out = out - wt[2, x - 1, z, out_at, :] * Q[f, x, z, at, :]
                out = out - wt[3, x - 1, z, out_at, :] * Q[f, x - 1, z, up, :]
                out = out - wt[4, x - 1, z, out_at, :] * Q[f, x - 1, z, dn, :]
                W[f, x - 1, z, out_at, :] = out
                q[z], w[z] = mid_v, out
            qs.append(q)
            ws.append(w)
        add_grams(2 * NP, qs, qs)
        add_grams(3 * NP, qs, ws)

    def face_tile(d, z, t, grams):
        x = 0 if d == 0 else cx - 1
        y = pl.multiple_of(t * TILE, TILE)
        at, out_at = pl.ds(y + TILE, TILE), pl.ds(y, TILE)
        face = wt[1 + d, x, z, out_at, :]
        vs = [face * qx[d, f, z, out_at, :] for f in range(F)]
        for f in range(F):
            W[f, x, z, out_at, :] = W[f, x, z, out_at, :] - vs[f]
        if grams:
            qs = [Q[f, x, z, at, :] for f in range(F)]
            for k, (i, j) in enumerate(PAIRS):
                acc[3 * NP + k] = acc[3 * NP + k] - (qs[i] * vs[j] + vs[i] * qs[j])

    def face(d, z, grams):
        @pl.when((has_lo, has_hi)[d])
        def _():
            arrive(d, 1, z)
            loop(0, T, lambda t: face_tile(d, z, t, grams))

    every = list(range(Z))

    def middle(planes, tile, *rest):
        lo, hi = planes
        def plane(x):
            for t in range(1, T - 1):
                tile(x, t, every, *rest)
        loop(lo, hi, plane)

    def rims(planes, tile, *rest):
        lo, hi = planes
        def plane(x):
            for t in (0, T - 1):
                tile(x, t, every, *rest)
        loop(lo, hi, plane)

    def chunk(z):
        for d, there in ((0, has_lo), (1, has_hi)):
            @pl.when(there)
            def _():
                arrive(d, 0, z)
        if z == 0:
            loop(0, 2, lambda k: spike(k * (cx + 1)))
        def plane(k):
            for t in range(T):
                first_tile(1 + k * (cx - 1), t, [z])
        loop(0, 2, plane)

    def forward_all(k, zs, ds=(0, 1)):
        for z in zs:
            for d in ds:
                forward(d, k, z)

    firsts = (first_up, first_dn)
    late = [(d, z) for z in order for d in (0, 1) if z not in firsts[d]]
    early = [(d, z) for z in order for d in (0, 1) if z in firsts[d]]
    split = (cx + 2) // 2
    middle((2, split), first_tile)
    middle((split, cx), first_tile)
    y_arrive((0, 1))
    forward_all(0, relay_0[:1])
    rims((2, cx), first_tile)
    y_send((2,))
    forward_all(0, relay_0[1:])
    middle((3, cx - 1), second_tile, True, True)
    for n, z in enumerate(order):
        if n == 2:
            y_arrive((2,))
            rims((3, cx - 1), second_tile, True, True)
        if n == Z - 1:
            for d in (0, 1):
                @pl.when(sides[d][1])
                def _():
                    take(wt.at[0, pl.ds(0, F + 1)], xs.at[d, 0])
                for c in order[:n]:
                    if c in firsts[d]:
                        send_direct(d, 1, c)
        chunk(z)
        for d in (0, 1):
            send_relayed(d, 1, z)
    for d in (0, 1):
        if order[Z - 1] in firsts[d]:
            send_direct(d, 1, order[Z - 1])
    y_send((3, 4))

    def beside_ends(k):
        for t in range(T):
            second_tile(2 + k * (cx - 3), t, every, True, True)
    loop(0, 2, beside_ends)
    for d, z in early:
        forward(d, 1, z)
    middle((1, 2), second_tile, False, True)
    middle((cx, cx + 1), second_tile, True, False)
    y_arrive((3, 4))
    rims((1, 2), second_tile, False, True)
    rims((cx, cx + 1), second_tile, True, False)
    for d, z in early:
        face(d, z, True)

    def compact(parts):
        lane_sum = jnp.sum(parts, axis=1, keepdims=True)
        out = jnp.zeros((TILE, LANES), jnp.float32)
        for k in range(4 * NP // TILE):
            out = jnp.where(lane == k, lane_sum[k * TILE:(k + 1) * TILE], out)
        return out

    part_x[mx] = compact(jnp.sum(acc[...], axis=1))

    def exchange(buf, axis, me, n, sends, recvs):
        for d in range(1, n):
            remote(buf.at[me], buf.at[me], sends.at[0], recvs.at[0], axis, lax.rem(me + d, n)).start()

    def gather(buf, n, recvs):
        if n > 1:
            take(buf.at[pl.ds(0, n - 1)], recvs.at[0])
        total = buf[0]
        for k in range(1, n):
            total = total + buf[k]
        return total

    exchange(part_x, "gx", mx, nx, ax_s, ax_r)
    for d, z in late[:half]:
        forward(d, 1, z)
    for d, z in late:
        send_direct(d, 1, z)
    part_y[my] = gather(part_x, nx, ax_r)
    exchange(part_y, "gy", my, ny, ay_s, ay_r)
    for d, z in late[half:]:
        forward(d, 1, z)
    for d, z in late:
        face(d, z, False)
    sums[...] = gather(part_y, ny, ay_r)

    if nx > 1:
        take(part_x.at[pl.ds(0, nx - 1)], ax_s.at[0])
    if ny > 1:
        take(part_y.at[pl.ds(0, ny - 1)], ay_s.at[0])
    for d in (0, 1):
        @pl.when(sides[d][1])
        def _():
            take(W.at[0, pl.ds(0, F)], xs.at[d, 1])

        @pl.when((y_hi, y_lo)[d])
        def _():
            take(wt.at[0, :, :, pl.ds(0, 2 * F + 1), :], ys.at[d])

    if relay_0 and relay_1:
        @pl.when(up_end | dn_end)
        def _():
            take(relay_r.at[pl.ds(0, len(relay_0))], fs.at[0])
            take(relay_q.at[pl.ds(0, len(relay_1))], fs.at[1])


def mat(a, b):
    return [
        [sum(a[i][k] * b[k][j] for k in range(1, F)) + a[i][0] * b[0][j] for j in range(F)]
        for i in range(F)
    ]


def add(a, b):
    return [[a[i][j] + b[i][j] for j in range(F)] for i in range(F)]


def sub(a, b):
    return [[a[i][j] - b[i][j] for j in range(F)] for i in range(F)]


def turn(a):
    return [[a[j][i] for j in range(F)] for i in range(F)]


def spd_solve(a, b):
    low = [[None] * F for _ in range(F)]
    inv = [None] * F
    rest = [list(row) for row in a]
    for k in range(F):
        inv[k] = 1.0 / rest[k][k]
        for i in range(k + 1, F):
            low[i][k] = rest[i][k] * inv[k]
        for i in range(k + 1, F):
            for j in range(k + 1, i + 1):
                rest[i][j] = rest[i][j] - low[i][k] * rest[j][k]
    out = [list(row) for row in b]
    for i in range(F):
        for k in range(i):
            out[i] = [u - low[i][k] * v for u, v in zip(out[i], out[k])]
    out = [[u * inv[i] for u in out[i]] for i in range(F)]
    for i in reversed(range(F)):
        for k in range(i + 1, F):
            out[i] = [u - low[k][i] * v for u, v in zip(out[i], out[k])]
    return out


def finish_kernel(sums, r_ref, q_ref, w_ref, x_out, e_out, x_ref, e_ref, coef, sems):
    def prepare():
        lane = lax.broadcasted_iota(jnp.int32, (TILE, LANES), 1)
        rows = []
        for k in range(4 * NP // TILE):
            column = jnp.sum(jnp.where(lane == k, sums[...], 0.0), axis=1, keepdims=True)
            wide = jnp.broadcast_to(column, (TILE, LANES))
            rows.extend(wide[s:s + 1] for s in range(TILE))
        grams = []
        for g in range(4):
            m = [[None] * F for _ in range(F)]
            for k, (i, j) in enumerate(PAIRS):
                m[i][j] = m[j][i] = rows[g * NP + k]
            grams.append(m)
        s0, s1, s2, s3 = grams
        a0 = spd_solve(s1, s0)
        s1a, s2a = mat(s1, a0), mat(s2, a0)
        a0t = turn(a0)
        rr = add(sub(sub(s0, s1a), turn(s1a)), mat(a0t, s2a))
        cross = add(sub(sub(s1, s2a), turn(s2a)), mat(a0t, mat(s3, a0)))
        beta = spd_solve(s0, rr)
        curve = sub(cross, mat(turn(beta), mat(s1, beta)))
        a1 = spd_solve(curve, rr)
        m1 = add(add(a0, a1), mat(beta, a1))
        m2 = mat(a0, a1)
        zero = jnp.zeros_like(m1[0][0])
        one = zero + 1.0
        weights = []
        for j in range(F):
            weights.append([m1[i][j] + m1[i][j] for i in range(F)] + [-(m2[i][j] + m2[i][j]) for i in range(F)] + [zero] * F)
        for j in range(F):
            unit = [one if i == j else zero for i in range(F)]
            weights.append(unit + [-m1[i][j] for i in range(F)] + [m2[i][j] for i in range(F)])
        depth = 3 * F * TILE
        row_s = lax.broadcasted_iota(jnp.int32, (TILE, LANES), 0)
        blocks = [[None] * 2 for _ in weights]
        for h in range(2):
            column = lane + h * LANES
            column = jnp.where(column >= depth, column - depth, column)
            at = [column == k * TILE + row_s for k in range(3 * F)]
            for j, row in enumerate(weights):
                block = jnp.zeros((TILE, LANES), jnp.float32)
                for k in range(3 * F):
                    if row[k] is not zero:
                        block = jnp.where(at[k], jnp.broadcast_to(row[k], block.shape), block)
                blocks[j][h] = block
        full = jnp.concatenate([jnp.concatenate(pair, axis=1) for pair in blocks], axis=0)[:, :2 * depth]
        high = full.astype(jnp.bfloat16)
        low = (full - high.astype(jnp.float32)).astype(jnp.bfloat16)
        coef[...] = jnp.concatenate([high, low], axis=0)

    prepare()
    cx, Z, cy = w_ref.shape[1:4]
    wide = 2 if Z % 2 == 0 else 1

    def tile(x, t):
        y, wide_y = pl.ds(t * TILE, TILE), pl.ds(t * TILE + TILE, TILE)
        for z in range(0, Z, wide):
            stack = []
            for n in range(z, z + wide):
                stack.append(jnp.concatenate(
                    [r_ref[f, x + 1, n, wide_y, :] for f in range(F)]
                    + [q_ref[f, x, n, wide_y, :] for f in range(F)]
                    + [w_ref[f, x, n, y, :] for f in range(F)], axis=0))
            fields = jnp.concatenate(stack, axis=1)
            high = fields.astype(jnp.bfloat16)
            low = (fields - high.astype(jnp.float32)).astype(jnp.bfloat16)
            both = jnp.concatenate([high, low], axis=0)
            out = jnp.dot(coef[...], both, preferred_element_type=jnp.float32)
            n_out = 2 * F * TILE
            out = out[:n_out] + out[n_out:]
            at = pl.ds(z * LANES, wide * LANES)
            for j in range(F):
                x_ref[j, x, y, at] = out[j * TILE:(j + 1) * TILE]
                e_ref[j, x, y, at] = out[(F + j) * TILE:(F + j + 1) * TILE]

    parts = 2 if cy % (2 * TILE) == 0 else 1
    part = cy // parts

    def out_copies(x, h):
        y = pl.ds(h * part, part)
        return (
            pltpu.make_async_copy(x_ref.at[:, x, y], x_out.at[:, x, y], sems.at[0, x, h]),
            pltpu.make_async_copy(e_ref.at[:, x, y], e_out.at[:, x, y], sems.at[1, x, h]),
        )

    def plane(x, c):
        for h in range(parts):
            for t in range(h * part // TILE, (h + 1) * part // TILE):
                tile(x, t)
            for copy in out_copies(x, h):
                copy.start()
        return c

    lax.fori_loop(0, cx, plane, 0)
    for x in range(cx):
        for h in range(parts):
            for copy in out_copies(x, h):
                copy.wait()


def shards(nx, ny, adj, sig, elec):
    cx, cy, cz = sig.shape
    Z = cz // LANES
    current = math.sqrt(nx * cx * ny * cy * cz)
    block = jax.ShapeDtypeStruct(adj.shape, jnp.float32)
    hbm = pl.BlockSpec(memory_space=pltpu.HBM)
    vmem = pl.BlockSpec(memory_space=pltpu.VMEM)
    tall = cy + 2 * TILE
    f32 = lambda *dims: pltpu.VMEM(dims, jnp.float32)
    shape = lambda *dims: jax.ShapeDtypeStruct(dims, jnp.float32)
    dma = pltpu.SemaphoreType.DMA
    adj = pltpu.with_memory_space_constraint(adj, pltpu.HBM)
    sig = pltpu.with_memory_space_constraint(sig, pltpu.HBM)
    elec = pltpu.with_memory_space_constraint(elec, pltpu.HBM)
    slots = max(Z // 2, 1)
    r, q, w, sums = pl.pallas_call(
        functools.partial(operator_kernel, nx, ny, current),
        out_shape=(
            shape(F, cx + 2, Z, tall, LANES), shape(F, cx, Z, tall, LANES), shape(F, cx, Z, cy, LANES),
            shape(TILE, LANES),
        ),
        in_specs=[hbm, hbm, hbm],
        out_specs=(vmem, vmem, vmem, vmem),
        scratch_shapes=[
            pltpu.SMEM((F,), jnp.int32),
            f32(cx + 2, Z, tall, LANES),
            f32(7, cx, Z, cy, LANES),
            f32(2, F, Z, cy, LANES),
            f32(slots, F + 1, cy, LANES),
            f32(slots, F, cy, LANES),
            f32(4 * NP, TILE, LANES),
            f32(nx, TILE, LANES),
            f32(ny, TILE, LANES),
            dma((3,)), dma((2, 2)), dma((2, 2, Z)), dma((2, slots)), dma((2,)),
            dma((2,)), dma((2, 5)),
            dma((1,)), dma((1,)), dma((1,)), dma((1,)),
        ],
        compiler_params=pltpu.CompilerParams(collective_id=0, has_side_effects=True, vmem_limit_bytes=GRANT_A),
    )(adj, sig, elec)
    return pl.pallas_call(
        finish_kernel,
        out_shape=(block, block),
        in_specs=[vmem, vmem, vmem, vmem],
        out_specs=(hbm, hbm),
        scratch_shapes=[
            f32(F, cx, cy, cz), f32(F, cx, cy, cz),
            pltpu.VMEM((4 * F * TILE, 6 * F * TILE), jnp.bfloat16),
            dma((2, cx, 2)),
        ],
        compiler_params=pltpu.CompilerParams(vmem_limit_bytes=GRANT_B),
    )(sums, r, q, w)


def solution(mesh):
    placed = (P(None, "gx", "gy", None), P("gx", "gy", None), P())
    return jax.shard_map(
        functools.partial(shards, mesh.shape["gx"], mesh.shape["gy"]),
        mesh=mesh,
        in_specs=placed,
        out_specs=(P(None, "gx", "gy", None), P(None, "gx", "gy", None)),
        check_vma=False,
    )
```

```python
import functools
import math

import jax
import jax.numpy as jnp
from jax import lax
from jax.experimental import pallas as pl
from jax.experimental.pallas import tpu as pltpu
from jax.sharding import PartitionSpec as P

MESH = pl.DeviceIdType.MESH
F = 4
PAIRS = [(i, j) for i in range(F) for j in range(i, F)]
NP = len(PAIRS)
TILE = 8
GRANT_A = 16 * 1024 * 1024
GRANT_B = 12 * 1024 * 1024
LANES = 128


def remote(src, dst, send, recv, axis, index):
    return pltpu.make_async_remote_copy(
        src_ref=src, dst_ref=dst, send_sem=send, recv_sem=recv,
        device_id={axis: index}, device_id_type=MESH,
    )


def operator_kernel(
    nx, ny, current, adj, sig, elec_ref, R, Q, W, sums,
    elec, S, wt, qx, relay_r, relay_q, acc, part_x, part_y,
    local, xs, xr, hr, fs, ys, yr, ax_s, ax_r, ay_s, ay_r,
):
    cx, cy, cz = sig.shape
    Z = cz // LANES
    T = cy // TILE
    total_y = ny * cy
    mx, my = lax.axis_index("gx"), lax.axis_index("gy")
    barrier = pltpu.get_barrier_semaphore()
    rows = pl.ds(TILE, cy)
    inner = pl.ds(1, cx)

    for axis, me, n in (("gx", mx, nx), ("gy", my, ny)):
        for d in range(1, n):
            pl.semaphore_signal(
                barrier, inc=1, device_id={axis: lax.rem(me + d, n)}, device_id_type=MESH
            )

    loads = [pltpu.make_async_copy(elec_ref, elec, local.at[2])]
    for z in range(Z):
        at = pl.ds(z * LANES, LANES)
        loads.append(pltpu.make_async_copy(adj.at[:, :, :, at], R.at[:, inner, z, rows, :], local.at[0]))
        loads.append(pltpu.make_async_copy(sig.at[:, :, at], S.at[inner, z, rows, :], local.at[1]))
    for load in loads:
        load.start()

    has_lo, has_hi = mx > 0, mx < nx - 1
    below, above = jnp.maximum(mx - 1, 0), jnp.minimum(mx + 1, nx - 1)
    y_lo, y_hi = my > 0, my < ny - 1
    left, right = jnp.maximum(my - 1, 0), jnp.minimum(my + 1, ny - 1)

    def take(ref, sem):
        pltpu.make_async_copy(ref, ref, sem).wait()

    half = Z // 2
    mid = nx // 2
    relaying = nx >= 4
    order = [z for k in range(half) for z in (k, Z - 1 - k)] + ([half] if Z % 2 else [])
    first_up = [z for k, z in enumerate(order) if k % 4 in (0, 3)]
    first_dn = [z for z in order if z not in first_up]
    relay_0 = order[Z - half:] if relaying else []
    relay_1 = order[:half] if relaying else []
    up_cross, dn_cross = mx == mid - 1, mx == mid
    up_end, dn_end = mx == nx - 1, mx == 0

    def lanes(z):
        return pl.ds(z * LANES, LANES)

    def hop(d, k, z, axis_to):
        plane = cx - 1 if d == 0 else 0
        halo = 0 if d == 0 else cx + 1
        if k == 0:
            pairs = [
                (adj.at[:, plane, :, lanes(z)], R.at[:, halo, z, rows, :]),
                (sig.at[plane, :, lanes(z)], S.at[halo, z, rows, :]),
            ]
        else:
            pairs = [(Q.at[:, plane, z, rows, :], qx.at[d, :, z])]
        return [remote(src, dst, xs.at[d, k], xr.at[d, k, z], "gx", axis_to) for src, dst in pairs]

    def to_relay(d, k, z):
        plane = cx - 1 if d == 0 else 0
        end = nx - 1 if d == 0 else 0
        if k == 0:
            at = relay_0.index(z)
            pairs = [
                (adj.at[:, plane, :, lanes(z)], relay_r.at[at, pl.ds(0, F)]),
                (sig.at[plane, :, lanes(z)], relay_r.at[at, F]),
            ]
        else:
            at = relay_1.index(z)
            pairs = [(Q.at[:, plane, z, rows, :], relay_q.at[at])]
        return [remote(src, dst, xs.at[d, k], hr.at[k, at], "gx", end) for src, dst in pairs]

    def from_relay(d, k, z):
        halo = 0 if d == 0 else cx + 1
        target = mid if d == 0 else mid - 1
        if k == 0:
            at = relay_0.index(z)
            pairs = [
                (relay_r.at[at, pl.ds(0, F)], R.at[:, halo, z, rows, :]),
                (relay_r.at[at, F], S.at[halo, z, rows, :]),
            ]
        else:
            pairs = [(relay_q.at[relay_1.index(z)], qx.at[d, :, z])]
        return [remote(src, dst, fs.at[k], xr.at[d, k, z], "gx", target) for src, dst in pairs]

    sides = ((0, has_hi, above, up_cross, up_end), (1, has_lo, below, dn_cross, dn_end))

    def start(copies):
        for copy in copies:
            copy.start()

    def send_relayed(d, k, z):
        if z in (relay_0, relay_1)[k]:
            @pl.when(sides[d][3])
            def _():
                start(to_relay(d, k, z))

    def send_direct(d, k, z):
        _, there, to, cross, _ = sides[d]
        if z in (relay_0, relay_1)[k]:
            there = there & jnp.logical_not(cross)

        @pl.when(there)
        def _():
            start(hop(d, k, z, to))

    def forward(d, k, z):
        if z in (relay_0, relay_1)[k]:
            @pl.when(sides[d][4])
            def _():
                at = (relay_0, relay_1)[k].index(z)
                take((relay_r, relay_q)[k].at[at], hr.at[k, at])
                start(from_relay(d, k, z))

    def arrive(d, k, z):
        take((relay_r, relay_q)[k].at[0], xr.at[d, k, z])

    def y_hop(d, k):
        src_row, dst_row = (TILE + cy - 1, TILE - 1) if d == 0 else (TILE, TILE + cy)
        to = right if d == 0 else left
        if k == 0:
            src, dst = R.at[:, inner, :, src_row, :], R.at[:, inner, :, dst_row, :]
        elif k == 1:
            src, dst = S.at[inner, :, src_row, :], S.at[inner, :, dst_row, :]
        elif k == 2:
            span = pl.ds(1, cx - 2)
            src, dst = Q.at[:, span, :, src_row, :], Q.at[:, span, :, dst_row, :]
        else:
            x = 0 if k == 3 else cx - 1
            src, dst = Q.at[:, x, :, src_row, :], Q.at[:, x, :, dst_row, :]
        return remote(src, dst, ys.at[d], yr.at[d, k], "gy", to)

    def y_send(kinds):
        for d, there in ((0, y_hi), (1, y_lo)):
            @pl.when(there)
            def _():
                for k in kinds:
                    y_hop(d, k).start()

    def y_arrive(kinds):
        for d, there in ((0, y_lo), (1, y_hi)):
            @pl.when(there)
            def _():
                for k in kinds:
                    y_hop(d, k).wait_recv()

    pl.semaphore_wait(barrier, nx + ny - 2)
    for z in order:
        for d in (0, 1):
            send_relayed(d, 0, z)
    for z in order:
        for d in (0, 1):
            send_direct(d, 0, z)

    acc[...] = jnp.zeros_like(acc)
    nothing = jnp.zeros((cy, LANES), jnp.float32)
    no_row = jnp.zeros((1, LANES), jnp.float32)
    take(W, local.at[0])
    take(wt.at[0], local.at[1])
    loads[0].wait()

    row_id = lax.broadcasted_iota(jnp.int32, (cy, LANES), 0)
    first = lax.broadcasted_iota(jnp.int32, (cy, LANES), 1) == 0

    def spike(x):
        cell = row_id + ((mx * cx + x - 1) * total_y + my * cy)
        for f in range(F):
            here = jnp.where(first & (cell == elec[f]), current, 0.0)
            R[f, x, 0, rows, :] = R[f, x, 0, rows, :] + here

    def loop(lo, hi, body):
        def one(k, c):
            body(k)
            return c
        lax.fori_loop(lo, hi, one, 0)

    loop(1, cx + 1, spike)
    y_send((0, 1))

    for there, halo, own in ((has_lo, 0, 1), (has_hi, cx + 1, cx)):
        @pl.when(jnp.logical_not(there))
        def _():
            for z in range(Z):
                S[halo, z, rows, :] = S[own, z, rows, :]
                for f in range(F):
                    R[f, halo, z, rows, :] = nothing

    for there, halo, own in ((y_lo, TILE - 1, TILE), (y_hi, TILE + cy, TILE + cy - 1)):
        @pl.when(jnp.logical_not(there))
        def _():
            def fill(x):
                for z in range(Z):
                    S[x + 1, z, pl.ds(halo, 1), :] = S[x + 1, z, pl.ds(own, 1), :]
                    for f in range(F):
                        R[f, x + 1, z, pl.ds(halo, 1), :] = no_row
                        Q[f, x, z, pl.ds(halo, 1), :] = no_row
            loop(0, cx, fill)

    lane = lax.broadcasted_iota(jnp.int32, (TILE, LANES), 1)
    lane_lo, lane_hi = lane == 0, lane == LANES - 1

    def beside(get, zs, edge):
        blocks, fwd, bwd = {}, {}, {}
        for z in zs:
            for n in (z - 1, z, z + 1):
                if 0 <= n < Z and n not in blocks:
                    blocks[n] = get(n)
        for z in zs:
            for n in (z - 1, z):
                if n in blocks and n not in fwd:
                    fwd[n] = pltpu.roll(blocks[n], 1, axis=1)
            for n in (z, z + 1):
                if n in blocks and n not in bwd:
                    bwd[n] = pltpu.roll(blocks[n], LANES - 1, axis=1)
        out = {}
        for z in zs:
            before = fwd[z - 1] if z > 0 else edge(blocks[z])
            after = bwd[z + 1] if z < Z - 1 else edge(blocks[z])
            out[z] = (
                blocks[z],
                jnp.where(lane_lo, before, fwd[z]),
                jnp.where(lane_hi, after, bwd[z]),
            )
        return out

    def add_grams(base, lefts, rights):
        zs = list(lefts[0])
        for k, (i, j) in enumerate(PAIRS):
            total = None
            for z in zs:
                prod = lefts[i][z] * rights[j][z]
                total = prod if total is None else total + prod
            acc[base + k] = acc[base + k] + total

    def first_tile(x, t, zs):
        y = t * TILE
        at, up, dn = pl.ds(y + TILE, TILE), pl.ds(y + TILE - 1, TILE), pl.ds(y + TILE + 1, TILE)
        out_at = pl.ds(y, TILE)
        weights = {}
        near = beside(lambda z: S[x, z, at, :], zs, lambda v: v)
        for z in zs:
            here, zm, zp = near[z]
            faces = [
                here + S[x - 1, z, at, :], here + S[x + 1, z, at, :],
                here + S[x, z, up, :], here + S[x, z, dn, :], here + zm, here + zp,
            ]
            diag = ((faces[0] + faces[1]) + (faces[2] + faces[3])) + (faces[4] + faces[5])
            weights[z] = [diag] + faces
            for k in range(7):
                wt[k, x - 1, z, out_at, :] = weights[z][k]
        rs, qs = [], []
        for f in range(F):
            near = beside(lambda z: R[f, x, z, at, :], zs, jnp.zeros_like)
            r, q = {}, {}
            for z in zs:
                mid_v, zm, zp = near[z]
                d, wxm, wxp, wym, wyp, wzm, wzp = weights[z]
                out = d * mid_v - wzm * zm - wzp * zp
                out = out - wxm * R[f, x - 1, z, at, :] - wxp * R[f, x + 1, z, at, :]
                out = out - wym * R[f, x, z, up, :] - wyp * R[f, x, z, dn, :]
                Q[f, x - 1, z, at, :] = out
                r[z], q[z] = mid_v, out
            rs.append(r)
            qs.append(q)
        add_grams(0, rs, rs)
        add_grams(NP, rs, qs)

    def second_tile(x, t, zs, low, high):
        y = t * TILE
        at, up, dn = pl.ds(y + TILE, TILE), pl.ds(y + TILE - 1, TILE), pl.ds(y + TILE + 1, TILE)
        out_at = pl.ds(y, TILE)
        qs, ws = [], []
        for f in range(F):
            near = beside(lambda z: Q[f, x - 1, z, at, :], zs, jnp.zeros_like)
            q, w = {}, {}
            for z in zs:
                mid_v, zm, zp = near[z]
                out = wt[0, x - 1, z, out_at, :] * mid_v
                out = out - wt[5, x - 1, z, out_at, :] * zm - wt[6, x - 1, z, out_at, :] * zp
                if low:
                    out = out - wt[1, x - 1, z, out_at, :] * Q[f, x - 2, z, at, :]
                if high:
                    out = out - wt[2, x - 1, z, out_at, :] * Q[f, x, z, at, :]
                out = out - wt[3, x - 1, z, out_at, :] * Q[f, x - 1, z, up, :]
                out = out - wt[4, x - 1, z, out_at, :] * Q[f, x - 1, z, dn, :]
                W[f, x - 1, z, out_at, :] = out
                q[z], w[z] = mid_v, out
            qs.append(q)
            ws.append(w)
        add_grams(2 * NP, qs, qs)
        add_grams(3 * NP, qs, ws)

    def face_tile(d, z, t, grams):
        x = 0 if d == 0 else cx - 1
        y = pl.multiple_of(t * TILE, TILE)
        at, out_at = pl.ds(y + TILE, TILE), pl.ds(y, TILE)
        face = wt[1 + d, x, z, out_at, :]
        vs = [face * qx[d, f, z, out_at, :] for f in range(F)]
        for f in range(F):
            W[f, x, z, out_at, :] = W[f, x, z, out_at, :] - vs[f]
        if grams:
            qs = [Q[f, x, z, at, :] for f in range(F)]
            for k, (i, j) in enumerate(PAIRS):
                acc[3 * NP + k] = acc[3 * NP + k] - (qs[i] * vs[j] + vs[i] * qs[j])

    def face(d, z, grams):
        @pl.when((has_lo, has_hi)[d])
        def _():
            arrive(d, 1, z)
            loop(0, T, lambda t: face_tile(d, z, t, grams))

    every = list(range(Z))

    def middle(planes, tile, *rest):
        lo, hi = planes
        def plane(x):
            for t in range(1, T - 1):
                tile(x, t, every, *rest)
        loop(lo, hi, plane)

    def rims(planes, tile, *rest):
        lo, hi = planes
        def plane(x):
            for t in (0, T - 1):
                tile(x, t, every, *rest)
        loop(lo, hi, plane)

    def chunk(z):
        for d, there in ((0, has_lo), (1, has_hi)):
            @pl.when(there)
            def _():
                arrive(d, 0, z)
        if z == 0:
            loop(0, 2, lambda k: spike(k * (cx + 1)))
        def plane(k):
            for t in range(T):
                first_tile(1 + k * (cx - 1), t, [z])
        loop(0, 2, plane)

    def forward_all(k, zs, ds=(0, 1)):
        for z in zs:
            for d in ds:
                forward(d, k, z)

    firsts = (first_up, first_dn)
    late = [(d, z) for z in order for d in (0, 1) if z not in firsts[d]]
    early = [(d, z) for z in order for d in (0, 1) if z in firsts[d]]
    split = (cx + 2) // 2
    middle((2, split), first_tile)
    middle((split, cx), first_tile)
    y_arrive((0, 1))
    forward_all(0, relay_0[:1])
    rims((2, cx), first_tile)
    y_send((2,))
    forward_all(0, relay_0[1:])
    middle((3, cx - 1), second_tile, True, True)
    for n, z in enumerate(order):
        if n == 2:
            y_arrive((2,))
            rims((3, cx - 1), second_tile, True, True)
        if n == Z - 1:
            for d in (0, 1):
                @pl.when(sides[d][1])
                def _():
                    take(wt.at[0, pl.ds(0, F + 1)], xs.at[d, 0])
                for c in order[:n]:
                    if c in firsts[d]:
                        send_direct(d, 1, c)
        chunk(z)
        for d in (0, 1):
            send_relayed(d, 1, z)
    for d in (0, 1):
        if order[Z - 1] in firsts[d]:
            send_direct(d, 1, order[Z - 1])
    for d, c in late[:half]:
        send_direct(d, 1, c)
    y_send((3, 4))

    def beside_ends(k):
        for t in range(T):
            second_tile(2 + k * (cx - 3), t, every, True, True)
    loop(0, 2, beside_ends)
    for d, z in early:
        forward(d, 1, z)
    middle((1, 2), second_tile, False, True)
    middle((cx, cx + 1), second_tile, True, False)
    y_arrive((3, 4))
    rims((1, 2), second_tile, False, True)
    rims((cx, cx + 1), second_tile, True, False)
    for d, z in late[:half]:
        forward(d, 1, z)
    for d, z in early:
        face(d, z, True)

    def compact(parts):
        lane_sum = jnp.sum(parts, axis=1, keepdims=True)
        out = jnp.zeros((TILE, LANES), jnp.float32)
        for k in range(4 * NP // TILE):
            out = jnp.where(lane == k, lane_sum[k * TILE:(k + 1) * TILE], out)
        return out

    part_x[mx] = compact(jnp.sum(acc[...], axis=1))

    def exchange(buf, axis, me, n, sends, recvs):
        for d in range(1, n):
            remote(buf.at[me], buf.at[me], sends.at[0], recvs.at[0], axis, lax.rem(me + d, n)).start()

    def gather(buf, n, recvs):
        if n > 1:
            take(buf.at[pl.ds(0, n - 1)], recvs.at[0])
        total = buf[0]
        for k in range(1, n):
            total = total + buf[k]
        return total

    exchange(part_x, "gx", mx, nx, ax_s, ax_r)
    for d, z in late[half:]:
        send_direct(d, 1, z)
    part_y[my] = gather(part_x, nx, ax_r)
    exchange(part_y, "gy", my, ny, ay_s, ay_r)
    for d, z in late[half:]:
        forward(d, 1, z)
    for d, z in late:
        face(d, z, False)
    sums[...] = gather(part_y, ny, ay_r)

    if nx > 1:
        take(part_x.at[pl.ds(0, nx - 1)], ax_s.at[0])
    if ny > 1:
        take(part_y.at[pl.ds(0, ny - 1)], ay_s.at[0])
    for d in (0, 1):
        @pl.when(sides[d][1])
        def _():
            take(W.at[0, pl.ds(0, F)], xs.at[d, 1])

        @pl.when((y_hi, y_lo)[d])
        def _():
            take(wt.at[0, :, :, pl.ds(0, 2 * F + 1), :], ys.at[d])

    if relay_0 and relay_1:
        @pl.when(up_end | dn_end)
        def _():
            take(relay_r.at[pl.ds(0, len(relay_0))], fs.at[0])
            take(relay_q.at[pl.ds(0, len(relay_1))], fs.at[1])


def mat(a, b):
    return [
        [sum(a[i][k] * b[k][j] for k in range(1, F)) + a[i][0] * b[0][j] for j in range(F)]
        for i in range(F)
    ]


def add(a, b):
    return [[a[i][j] + b[i][j] for j in range(F)] for i in range(F)]


def sub(a, b):
    return [[a[i][j] - b[i][j] for j in range(F)] for i in range(F)]


def turn(a):
    return [[a[j][i] for j in range(F)] for i in range(F)]


def spd_solve(a, b):
    low = [[None] * F for _ in range(F)]
    inv = [None] * F
    rest = [list(row) for row in a]
    for k in range(F):
        inv[k] = 1.0 / rest[k][k]
        for i in range(k + 1, F):
            low[i][k] = rest[i][k] * inv[k]
        for i in range(k + 1, F):
            for j in range(k + 1, i + 1):
                rest[i][j] = rest[i][j] - low[i][k] * rest[j][k]
    out = [list(row) for row in b]
    for i in range(F):
        for k in range(i):
            out[i] = [u - low[i][k] * v for u, v in zip(out[i], out[k])]
    out = [[u * inv[i] for u in out[i]] for i in range(F)]
    for i in reversed(range(F)):
        for k in range(i + 1, F):
            out[i] = [u - low[k][i] * v for u, v in zip(out[i], out[k])]
    return out


def finish_kernel(sums, r_ref, q_ref, w_ref, x_out, e_out, x_ref, e_ref, coef, sems):
    def prepare():
        lane = lax.broadcasted_iota(jnp.int32, (TILE, LANES), 1)
        rows = []
        for k in range(4 * NP // TILE):
            column = jnp.sum(jnp.where(lane == k, sums[...], 0.0), axis=1, keepdims=True)
            wide = jnp.broadcast_to(column, (TILE, LANES))
            rows.extend(wide[s:s + 1] for s in range(TILE))
        grams = []
        for g in range(4):
            m = [[None] * F for _ in range(F)]
            for k, (i, j) in enumerate(PAIRS):
                m[i][j] = m[j][i] = rows[g * NP + k]
            grams.append(m)
        s0, s1, s2, s3 = grams
        a0 = spd_solve(s1, s0)
        s1a, s2a = mat(s1, a0), mat(s2, a0)
        a0t = turn(a0)
        rr = add(sub(sub(s0, s1a), turn(s1a)), mat(a0t, s2a))
        cross = add(sub(sub(s1, s2a), turn(s2a)), mat(a0t, mat(s3, a0)))
        beta = spd_solve(s0, rr)
        curve = sub(cross, mat(turn(beta), mat(s1, beta)))
        a1 = spd_solve(curve, rr)
        m1 = add(add(a0, a1), mat(beta, a1))
        m2 = mat(a0, a1)
        zero = jnp.zeros_like(m1[0][0])
        one = zero + 1.0
        weights = []
        for j in range(F):
            weights.append([m1[i][j] + m1[i][j] for i in range(F)] + [-(m2[i][j] + m2[i][j]) for i in range(F)] + [zero] * F)
        for j in range(F):
            unit = [one if i == j else zero for i in range(F)]
            weights.append(unit + [-m1[i][j] for i in range(F)] + [m2[i][j] for i in range(F)])
        depth = 3 * F * TILE
        row_s = lax.broadcasted_iota(jnp.int32, (TILE, LANES), 0)
        blocks = [[None] * 2 for _ in weights]
        for h in range(2):
            column = lane + h * LANES
            column = jnp.where(column >= depth, column - depth, column)
            at = [column == k * TILE + row_s for k in range(3 * F)]
            for j, row in enumerate(weights):
                block = jnp.zeros((TILE, LANES), jnp.float32)
                for k in range(3 * F):
                    if row[k] is not zero:
                        block = jnp.where(at[k], jnp.broadcast_to(row[k], block.shape), block)
                blocks[j][h] = block
        full = jnp.concatenate([jnp.concatenate(pair, axis=1) for pair in blocks], axis=0)[:, :2 * depth]
        high = full.astype(jnp.bfloat16)
        low = (full - high.astype(jnp.float32)).astype(jnp.bfloat16)
        coef[...] = jnp.concatenate([high, low], axis=0)

    prepare()
    cx, Z, cy = w_ref.shape[1:4]
    wide = 2 if Z % 2 == 0 else 1

    def tile(x, t):
        y, wide_y = pl.ds(t * TILE, TILE), pl.ds(t * TILE + TILE, TILE)
        for z in range(0, Z, wide):
            stack = []
            for n in range(z, z + wide):
                stack.append(jnp.concatenate(
                    [r_ref[f, x + 1, n, wide_y, :] for f in range(F)]
                    + [q_ref[f, x, n, wide_y, :] for f in range(F)]
                    + [w_ref[f, x, n, y, :] for f in range(F)], axis=0))
            fields = jnp.concatenate(stack, axis=1)
            high = fields.astype(jnp.bfloat16)
            low = (fields - high.astype(jnp.float32)).astype(jnp.bfloat16)
            both = jnp.concatenate([high, low], axis=0)
            out = jnp.dot(coef[...], both, preferred_element_type=jnp.float32)
            n_out = 2 * F * TILE
            out = out[:n_out] + out[n_out:]
            at = pl.ds(z * LANES, wide * LANES)
            for j in range(F):
                x_ref[j, x, y, at] = out[j * TILE:(j + 1) * TILE]
                e_ref[j, x, y, at] = out[(F + j) * TILE:(F + j + 1) * TILE]

    parts = 4 if cy % (4 * TILE) == 0 else 1
    part = cy // parts

    def out_copies(x, h):
        y = pl.ds(h * part, part)
        return (
            pltpu.make_async_copy(x_ref.at[:, x, y], x_out.at[:, x, y], sems.at[0]),
            pltpu.make_async_copy(e_ref.at[:, x, y], e_out.at[:, x, y], sems.at[1]),
        )

    def plane(x, c):
        for h in range(parts):
            for t in range(h * part // TILE, (h + 1) * part // TILE):
                tile(x, t)
            for copy in out_copies(x, h):
                copy.start()
        return c

    lax.fori_loop(0, cx, plane, 0)
    pltpu.make_async_copy(x_ref, x_out, sems.at[0]).wait()
    pltpu.make_async_copy(e_ref, e_out, sems.at[1]).wait()


def shards(nx, ny, adj, sig, elec):
    cx, cy, cz = sig.shape
    Z = cz // LANES
    current = math.sqrt(nx * cx * ny * cy * cz)
    block = jax.ShapeDtypeStruct(adj.shape, jnp.float32)
    hbm = pl.BlockSpec(memory_space=pltpu.HBM)
    vmem = pl.BlockSpec(memory_space=pltpu.VMEM)
    tall = cy + 2 * TILE
    f32 = lambda *dims: pltpu.VMEM(dims, jnp.float32)
    shape = lambda *dims: jax.ShapeDtypeStruct(dims, jnp.float32)
    dma = pltpu.SemaphoreType.DMA
    adj = pltpu.with_memory_space_constraint(adj, pltpu.HBM)
    sig = pltpu.with_memory_space_constraint(sig, pltpu.HBM)
    elec = pltpu.with_memory_space_constraint(elec, pltpu.HBM)
    slots = max(Z // 2, 1)
    r, q, w, sums = pl.pallas_call(
        functools.partial(operator_kernel, nx, ny, current),
        out_shape=(
            shape(F, cx + 2, Z, tall, LANES), shape(F, cx, Z, tall, LANES), shape(F, cx, Z, cy, LANES),
            shape(TILE, LANES),
        ),
        in_specs=[hbm, hbm, hbm],
        out_specs=(vmem, vmem, vmem, vmem),
        scratch_shapes=[
            pltpu.SMEM((F,), jnp.int32),
            f32(cx + 2, Z, tall, LANES),
            f32(7, cx, Z, cy, LANES),
            f32(2, F, Z, cy, LANES),
            f32(slots, F + 1, cy, LANES),
            f32(slots, F, cy, LANES),
            f32(4 * NP, TILE, LANES),
            f32(nx, TILE, LANES),
            f32(ny, TILE, LANES),
            dma((3,)), dma((2, 2)), dma((2, 2, Z)), dma((2, slots)), dma((2,)),
            dma((2,)), dma((2, 5)),
            dma((1,)), dma((1,)), dma((1,)), dma((1,)),
        ],
        compiler_params=pltpu.CompilerParams(collective_id=0, has_side_effects=True, vmem_limit_bytes=GRANT_A),
    )(adj, sig, elec)
    return pl.pallas_call(
        finish_kernel,
        out_shape=(block, block),
        in_specs=[vmem, vmem, vmem, vmem],
        out_specs=(hbm, hbm),
        scratch_shapes=[
            f32(F, cx, cy, cz), f32(F, cx, cy, cz),
            pltpu.VMEM((4 * F * TILE, 6 * F * TILE), jnp.bfloat16),
            dma((2,)),
        ],
        compiler_params=pltpu.CompilerParams(vmem_limit_bytes=GRANT_B),
    )(sums, r, q, w)


def solution(mesh):
    placed = (P(None, "gx", "gy", None), P("gx", "gy", None), P())
    return jax.shard_map(
        functools.partial(shards, mesh.shape["gx"], mesh.shape["gy"]),
        mesh=mesh,
        in_specs=placed,
        out_specs=(P(None, "gx", "gy", None), P(None, "gx", "gy", None)),
        check_vma=False,
    )
```
